32 devices in a mesh: fsdp: 4 (over y, x), ctx: 2 (over core), tp: 4 (over z).
Axes of the slice: x: 2, y: 2, z: 4, core: 2. Of those that a mesh axis runs over, the one named last changes fastest.
Arguments:
- block_input: float32 [4, 1024, 2048], P('fsdp', 'ctx'), may hold values from -6 to 6
- cotangent: float32 [4, 1024, 2048], P('fsdp', 'ctx'), may hold values from -6 to 6
- w_query: bfloat16 [2048, 2048], P(('fsdp', 'ctx'), 'tp'), may hold values from -0.125 to 0.125
- w_key: bfloat16 [2048, 512], P(('fsdp', 'ctx'), 'tp'), may hold values from -0.125 to 0.125
- w_value: bfloat16 [2048, 512], P(('fsdp', 'ctx'), 'tp'), may hold values from -0.125 to 0.125
- w_output: bfloat16 [2048, 2048], P('tp', ('fsdp', 'ctx')), may hold values from -4 to 4
- w_gate: bfloat16 [2048, 8192], P(('fsdp', 'ctx'), 'tp'), may hold values from -0.125 to 0.125
- w_up: bfloat16 [2048, 8192], P(('fsdp', 'ctx'), 'tp'), may hold values from -0.125 to 0.125
- w_down: bfloat16 [8192, 2048], P('tp', ('fsdp', 'ctx')), may hold values from -0.0625 to 0.0625
- attn_gain: bfloat16 [2048], P(('fsdp', 'ctx')), may hold values from 0.5 to 1.5
- ffn_gain: bfloat16 [2048], P(('fsdp', 'ctx')), may hold values from 0.5 to 1.5
Outputs:
- block_output: float32 [4, 1024, 2048], P('fsdp', 'ctx')
- input_grad: float32 [4, 1024, 2048], P('fsdp', 'ctx')
- grad_query: float32 [2048, 2048], P(('fsdp', 'ctx'), 'tp')
- grad_key: float32 [2048, 512], P(('fsdp', 'ctx'), 'tp')
- grad_value: float32 [2048, 512], P(('fsdp', 'ctx'), 'tp')
- grad_output: float32 [2048, 2048], P('tp', ('fsdp', 'ctx'))
- grad_gate: float32 [2048, 8192], P(('fsdp', 'ctx'), 'tp')
- grad_up: float32 [2048, 8192], P(('fsdp', 'ctx'), 'tp')
- grad_down: float32 [8192, 2048], P('tp', ('fsdp', 'ctx'))
- grad_attn_gain: float32 [2048], P(('fsdp', 'ctx'))
- grad_ffn_gain: float32 [2048], P(('fsdp', 'ctx'))
The draws below stay inside these ranges and needn't reach their ends.
All inputs are finite; a program needn't handle non-finite values.
Results may differ from the reference program's by a relative error of at most 0.013.
Values may be sent and summed in bfloat16 or wider, within the bound.
No kernel may reach another device: no remote copies, remote signals or barrier semaphores. Data moves between devices by JAX's collectives and lax.ppermute only.
A program may use at most 256 MiB of HBM per device.

```python
import jax
import jax.numpy as jnp
from jax import lax

D = 2048
HQ = 32
KV = 8
HD = 64
FF = 8192
SEQLEN = 1024
SEQS = 4


def level_of(key, shape, split, least, largest):
    def one(position, shards_of):
        draws = jax.random.uniform(jax.random.fold_in(jax.random.fold_in(key, 6), position), (shards_of,), jnp.float32, least / len(split), largest / len(split))
        return jnp.repeat(jnp.exp(draws), shape[position] // shards_of).reshape((-1,) + (1,) * (len(shape) - position - 1))

    factor_of = one(*split[0])
    for cut in split[1:]:
        factor_of = factor_of * one(*cut)
    return factor_of


def normal_values(stream_key, dims, spread, most, cuts=(), held_as=jnp.bfloat16):
    drawn = spread * jax.random.normal(stream_key, dims, jnp.float32)
    if cuts:
        drawn = drawn * level_of(stream_key, dims, cuts, -0.22, 0.18)
    return jnp.clip(drawn, -most, most).astype(held_as)


def setup_inputs(seed: int = 0) -> dict:
    key_list = jax.random.split(jax.random.key(seed), 12)
    block_input = normal_values(key_list[0], (SEQS, SEQLEN, D), 1.0, 6.0, ((0, 4), (1, 2)), jnp.float32)
    cotangent = normal_values(key_list[1], (SEQS, SEQLEN, D), 1.0, 6.0, ((0, 4), (1, 2)), jnp.float32)
    w_query = normal_values(key_list[2], (D, HQ * HD), D ** -0.5, 0.125, ((0, 8), (1, 4)))
    w_key = normal_values(key_list[3], (D, KV * HD), D ** -0.5, 0.125, ((0, 8), (1, 4)))
    w_value = normal_values(key_list[4], (D, KV * HD), D ** -0.5, 0.125, ((0, 8), (1, 4)))
    w_output = normal_values(key_list[5], (HQ * HD, D), (max(1, SEQLEN // 512)) ** -0.5, 4.0, ((0, 4), (1, 8)))
    w_gate = normal_values(key_list[6], (D, FF), D ** -0.5, 0.125, ((0, 8), (1, 4)))
    w_up = normal_values(key_list[7], (D, FF), D ** -0.5, 0.125, ((0, 8), (1, 4)))
    w_down = normal_values(key_list[8], (FF, D), FF ** -0.5, 0.0625, ((0, 4), (1, 8)))
    attn_gain = jnp.clip(1.0 + 0.1 * jax.random.normal(key_list[9], (D,), jnp.float32), 0.5, 1.5).astype(jnp.bfloat16)
    ffn_gain = jnp.clip(1.0 + 0.1 * jax.random.normal(key_list[10], (D,), jnp.float32), 0.5, 1.5).astype(jnp.bfloat16)
    return dict(block_input=block_input, cotangent=cotangent, w_query=w_query, w_key=w_key, w_value=w_value, w_output=w_output, w_gate=w_gate, w_up=w_up, w_down=w_down, attn_gain=attn_gain, ffn_gain=ffn_gain)


EPS = 1e-05
BASE = 500000.0
NEG = -1e+30

def rotate(values, positions, sign):
    half = values.shape[-1] // 2
    inverse = BASE ** (-(jnp.arange(half, dtype=jnp.float32) * 2.0) / values.shape[-1])
    angle = positions.astype(jnp.float32)[:, None] * inverse[None, :]
    cosine = jnp.cos(angle)[:, None, :]
    sine = sign * jnp.sin(angle)[:, None, :]
    first = values[..., :half]
    second = values[..., half:]
    return jnp.concatenate([first * cosine - second * sine, second * cosine + first * sine], axis=-1)

def norm_forward(rows, gain):
    scale = lax.rsqrt(lax.optimization_barrier(jnp.mean(rows * rows, axis=-1, keepdims=True)) + EPS)
    return (rows * scale * gain, scale)

def norm_backward(rows, scale, gain, grad):
    weighted = grad * gain
    d_rows = scale * weighted - rows * scale ** 3 * lax.optimization_barrier(jnp.mean(weighted * rows, axis=-1, keepdims=True))
    return (d_rows, lax.optimization_barrier(jnp.sum(grad * rows * scale, axis=0)))

def forward_block(queries, keys, vals, allow, scale):
    scores = jnp.einsum('gbd,kd->gbk', queries.astype(jnp.float32), keys.astype(jnp.float32)) * scale
    scores = jnp.where(allow[None], scores, NEG)
    top = lax.optimization_barrier(jnp.max(scores, axis=-1, keepdims=True))
    total = top[..., 0] + jnp.log(lax.optimization_barrier(jnp.sum(jnp.exp(scores - top), axis=-1)))
    probs = jnp.exp(scores - total[..., None]).astype(jnp.bfloat16)
    out = jnp.einsum('gbk,kd->gbd', probs.astype(jnp.float32), vals.astype(jnp.float32))
    return (out.astype(jnp.bfloat16), total)

def backward_block(queries, keys, vals, allow, total, grad_out, out, scale):
    scores = jnp.einsum('gbd,kd->gbk', queries.astype(jnp.float32), keys.astype(jnp.float32)) * scale
    scores = jnp.where(allow[None], scores, NEG)
    probs = jnp.exp(scores - total[..., None])
    rounded = probs.astype(jnp.bfloat16).astype(jnp.float32)
    grad_f = grad_out.astype(jnp.float32)
    d_vals = jnp.einsum('gbk,gbd->kd', rounded, grad_f)
    d_probs = jnp.einsum('gbd,kd->gbk', grad_f, vals.astype(jnp.float32))
    delta = lax.optimization_barrier(jnp.sum(grad_f * out.astype(jnp.float32), axis=-1))
    d_scores = (probs * (d_probs - delta[..., None]) * scale).astype(jnp.bfloat16).astype(jnp.float32)
    d_query = jnp.einsum('gbk,kd->gbd', d_scores, keys.astype(jnp.float32))
    d_keys = jnp.einsum('gbk,gbd->kd', d_scores, queries.astype(jnp.float32))
    return (d_query, d_keys, d_vals)

def split_blocks(tensor, count, block):
    return tensor.reshape((tensor.shape[0], count, block) + tensor.shape[2:]).swapaxes(0, 1)

def attention_forward(grouped, keys, vals, allow, block, scale):

    def per_head(items):
        head_q, head_k, head_v = items
        groups, rows, width = head_q.shape
        count = rows // block
        outs, totals = lax.map(lambda piece: forward_block(piece[0], head_k, head_v, piece[1], scale), (split_blocks(head_q, count, block), allow.reshape(count, block, allow.shape[1])))
        return (outs.swapaxes(0, 1).reshape(groups, rows, width), totals.swapaxes(0, 1).reshape(groups, rows))
    return lax.map(per_head, (grouped, keys, vals))

def attention_backward(grouped, keys, vals, allow, totals, grads, outs, block, scale):

    def per_head(items):
        head_q, head_k, head_v, head_t, head_g, head_o = items
        groups, rows, width = head_q.shape
        count = rows // block

        def step(carry, piece):
            d_query, d_keys, d_vals = backward_block(piece[0], head_k, head_v, piece[1], piece[2], piece[3], piece[4], scale)
            return ((carry[0] + d_keys, carry[1] + d_vals), d_query)
        zeros = jnp.zeros(head_k.shape, jnp.float32)
        pieces = (split_blocks(head_q, count, block), allow.reshape(count, block, allow.shape[1]), split_blocks(head_t, count, block), split_blocks(head_g, count, block), split_blocks(head_o, count, block))
        (d_keys, d_vals), d_query = lax.scan(step, (zeros, zeros), pieces)
        return (d_query.swapaxes(0, 1).reshape(groups, rows, width), d_keys, d_vals)
    return lax.map(per_head, (grouped, keys, vals, totals, grads, outs))

def dotf(left, right):
    return jnp.dot(left, right, preferred_element_type=jnp.float32)

def one_sequence(weights, rows, cot):
    w_query, w_key, w_value, w_output, w_gate, w_up, w_down, attn_gain, ffn_gain = weights
    length = rows.shape[0]
    groups = HQ // KV
    block = min(512, length)
    scale = HD ** (-0.5)
    positions = jnp.arange(length, dtype=jnp.int32)
    gain_a = attn_gain.astype(jnp.float32)
    gain_f = ffn_gain.astype(jnp.float32)
    normed_f, scale_a = norm_forward(rows, gain_a)
    normed = normed_f.astype(jnp.bfloat16)
    query = dotf(normed, w_query).reshape(length, HQ, HD)
    keys = dotf(normed, w_key).reshape(length, KV, HD)
    vals = dotf(normed, w_value).reshape(length, KV, HD)
    query_rot = rotate(query, positions, 1.0).astype(jnp.bfloat16)
    keys_rot = rotate(keys, positions, 1.0).astype(jnp.bfloat16).transpose(1, 0, 2)
    vals_b = vals.astype(jnp.bfloat16).transpose(1, 0, 2)
    grouped = query_rot.reshape(length, KV, groups, HD).transpose(1, 2, 0, 3)
    index = jnp.arange(length, dtype=jnp.int32)
    allow = index[None, :] <= index[:, None]
    attn, totals = attention_forward(grouped, keys_rot, vals_b, allow, block, scale)
    attn_flat = attn.transpose(2, 0, 1, 3).reshape(length, HQ * HD)
    hidden = rows + dotf(attn_flat, w_output)
    hnorm_f, scale_f = norm_forward(hidden, gain_f)
    hnorm = hnorm_f.astype(jnp.bfloat16)
    gate = dotf(hnorm, w_gate)
    up = dotf(hnorm, w_up)
    sigma = jax.nn.sigmoid(gate)
    active = gate * sigma
    inner = (active * up).astype(jnp.bfloat16)
    out = hidden + dotf(inner, w_down)
    cot_b = cot.astype(jnp.bfloat16)
    g_down = dotf(inner.T, cot_b)
    d_inner = dotf(cot_b, w_down.T)
    d_gate = (d_inner * up * sigma * (1.0 + gate * (1.0 - sigma))).astype(jnp.bfloat16)
    d_up = (d_inner * active).astype(jnp.bfloat16)
    g_gate = dotf(hnorm.T, d_gate)
    g_up = dotf(hnorm.T, d_up)
    d_hnorm = dotf(d_gate, w_gate.T) + dotf(d_up, w_up.T)
    d_norm, g_ffn = norm_backward(hidden, scale_f, gain_f, d_hnorm)
    d_hidden = cot + d_norm
    dh_b = d_hidden.astype(jnp.bfloat16)
    g_output = dotf(attn_flat.T, dh_b)
    d_attn = dotf(dh_b, w_output.T).astype(jnp.bfloat16).reshape(length, KV, groups, HD).transpose(1, 2, 0, 3)
    d_query, d_keys, d_vals = attention_backward(grouped, keys_rot, vals_b, allow, totals, d_attn, attn, block, scale)
    d_query = d_query.transpose(2, 0, 1, 3).reshape(length, HQ, HD)
    dq_b = rotate(d_query, positions, -1.0).astype(jnp.bfloat16).reshape(length, HQ * HD)
    dk_b = rotate(d_keys.transpose(1, 0, 2), positions, -1.0).astype(jnp.bfloat16).reshape(length, KV * HD)
    dv_b = d_vals.transpose(1, 0, 2).reshape(length, KV * HD).astype(jnp.bfloat16)
    g_query = dotf(normed.T, dq_b)
    g_key = dotf(normed.T, dk_b)
    g_value = dotf(normed.T, dv_b)
    d_normed = dotf(dq_b, w_query.T) + dotf(dk_b, w_key.T) + dotf(dv_b, w_value.T)
    d_rows, g_attn = norm_backward(rows, scale_a, gain_a, d_normed)
    d_input = d_hidden + d_rows
    return (out, d_input, (g_query, g_key, g_value, g_output, g_gate, g_up, g_down, g_attn, g_ffn))

def reference(block_input, cotangent, w_query, w_key, w_value, w_output, w_gate, w_up, w_down, attn_gain, ffn_gain):
    weights = (w_query, w_key, w_value, w_output, w_gate, w_up, w_down, attn_gain, ffn_gain)
    zeros = tuple((jnp.zeros(weight.shape, jnp.float32) for weight in weights))

    def step(carry, item):
        out, d_input, grads = one_sequence(weights, item[0], item[1])
        return (tuple((total + grad for total, grad in zip(carry, grads))), (out, d_input))
    sums, (outs, d_inputs) = lax.scan(step, zeros, (block_input, cotangent))
    return (outs, d_inputs, sums[0], sums[1], sums[2], sums[3], sums[4], sums[5], sums[6], sums[7], sums[8])
```

```python
import jax
import jax.numpy as jnp
from jax import lax
from jax.experimental import pallas as pl
from jax.experimental.pallas import tpu as pltpu
from jax.sharding import PartitionSpec as P

HD = 64
EPS = 1e-05
BASE = 500000.0
NEG = -1e30
BF = jnp.bfloat16
F32 = jnp.float32
BLOCK = 256


def dotf(left, right):
    return jnp.dot(left, right, preferred_element_type=F32)


def dot_t(left, right):
    return lax.dot_general(left, right, (((1,), (1,)), ((), ())), preferred_element_type=F32)


def dot_0(left, right):
    return lax.dot_general(left, right, (((0,), (0,)), ((), ())), preferred_element_type=F32)


def after(value, *others):
    return lax.optimization_barrier((value,) + others)[0]


def swap(value):
    return lax.ppermute(value, "ctx", [(0, 1), (1, 0)])


def pair(mine, theirs, core, axis):
    first = jnp.where(core == 0, mine, theirs)
    second = jnp.where(core == 0, theirs, mine)
    return jnp.concatenate([first, second], axis=axis)


def half_of(value, which, axis):
    size = value.shape[axis] // 2
    return lax.dynamic_slice_in_dim(value, which * size, size, axis)


def rotations(count):
    return [[(k, (k + s) % count) for k in range(count)] for s in range(1, count)]


def gather_tokens(piece):
    count = lax.axis_size("tp")
    return [piece] + [lax.ppermute(piece, "tp", pairs) for pairs in rotations(count)]


def scatter_tokens(pieces):
    count = lax.axis_size("tp")
    total = pieces[0].astype(F32)
    got = [
        lax.ppermute(pieces[(count - s) % count].astype(BF), "tp", pairs)
        for s, pairs in enumerate(rotations(count), 1)
    ]
    for item in got:
        total = total + item.astype(F32)
    return total


def to_rotated(rows, place, count):
    size = rows.shape[0] // count
    return [
        lax.dynamic_slice_in_dim(rows, ((place - s) % count) * size, size, 0) for s in range(count)
    ]


def from_rotated(pieces, place):
    count = len(pieces)
    stacked = jnp.concatenate(pieces, axis=0)
    size = pieces[0].shape[0]
    return jnp.concatenate(
        [
            lax.dynamic_slice_in_dim(stacked, ((place - j) % count) * size, size, 0)
            for j in range(count)
        ],
        axis=0,
    )


def gather_fsdp(shard):
    count = lax.axis_size("fsdp")
    if count != 4:
        return lax.all_gather(shard, "fsdp", axis=0, tiled=True)
    me = lax.axis_index("fsdp")
    near = [(k, k ^ 1) for k in range(4)]
    far = [(k, k ^ 2) for k in range(4)]
    size = shard.shape[0]
    cut = size // 32 * 16
    one = lax.ppermute(shard, "fsdp", near)
    two = lax.ppermute(shard, "fsdp", far)
    three_a = lax.ppermute(one[:cut], "fsdp", far)
    three_b = lax.ppermute(two[cut:], "fsdp", near)
    three = jnp.concatenate([three_a, three_b], axis=0)
    low = (me & 1) == 0
    high = (me & 2) == 0
    a, b = jnp.where(low, shard, one), jnp.where(low, one, shard)
    c, d = jnp.where(low, two, three), jnp.where(low, three, two)
    return jnp.concatenate(
        [jnp.where(high, a, c), jnp.where(high, b, d), jnp.where(high, c, a), jnp.where(high, d, b)],
        axis=0,
    )


def sum_everywhere(value):
    for pairs in rotations(lax.axis_size("tp")):
        pass
    got = [lax.ppermute(value, "tp", pairs) for pairs in rotations(lax.axis_size("tp"))]
    for item in got:
        value = value + item
    value = value + swap(value)
    count = lax.axis_size("fsdp")
    step = 1
    while step < count:
        value = value + lax.ppermute(value, "fsdp", [(k, k ^ step) for k in range(count)])
        step *= 2
    return value


def halves_swapped(tile):
    lane = lax.broadcasted_iota(jnp.int32, tile.shape, 1)
    width = tile.shape[1]
    back = pltpu.roll(tile, width - HD // 2, 1)
    ahead = pltpu.roll(tile, HD // 2, 1)
    return jnp.where(lane % HD < HD // 2, back, ahead)


def padded(kv):
    lane = lax.broadcasted_iota(jnp.int32, kv.shape, 1)
    low = lane < HD
    other = pltpu.roll(kv, HD, 1)
    zero = jnp.zeros_like(kv)
    keys = (jnp.where(low, kv, zero), jnp.where(low, zero, other))
    vals = (jnp.where(low, other, zero), jnp.where(low, zero, kv))
    return keys, vals


def attend_kernel(qkv_ref, cos_ref, sin_ref, cos_kv_ref, sin_kv_ref, q_ref, kv_ref, out_ref, lse_ref):
    tokens, width = out_ref.shape
    scale = HD ** (-0.5)
    tiles = width // 128
    for j in range(tiles):
        tile = qkv_ref[:, j * 128 : (j + 1) * 128]
        turned = tile * cos_ref[...] + halves_swapped(tile) * sin_ref[...]
        q_ref[:, j * 128 : (j + 1) * 128] = turned.astype(BF)
    tile = qkv_ref[:, width : width + 128]
    kv = tile * cos_kv_ref[...] + halves_swapped(tile) * sin_kv_ref[...]
    kv_ref[...] = kv.astype(BF)
    keys, vals = padded(kv)
    keys = [k.astype(BF) for k in keys]
    vals = [v.astype(BF) for v in vals]
    row = lax.broadcasted_iota(jnp.int32, (BLOCK, BLOCK), 0)
    col = lax.broadcasted_iota(jnp.int32, (BLOCK, BLOCK), 1)
    causal = col <= row
    for i in range(tokens // BLOCK):
        at = slice(i * BLOCK, (i + 1) * BLOCK)
        for j in range(tiles):
            queries = q_ref[at, j * 128 : (j + 1) * 128]
            result = None
            for side in range(2):
                key, val = keys[side], vals[side]
                diag = dot_t(queries, key[at]) * scale
                diag = jnp.where(causal, diag, NEG)
                top = jnp.max(diag, axis=-1, keepdims=True)
                if i:
                    past = dot_t(queries, key[: i * BLOCK]) * scale
                    top = jnp.maximum(top, jnp.max(past, axis=-1, keepdims=True))
                    weight = jnp.exp(past - top)
                p_diag = jnp.exp(diag - top)
                total = jnp.sum(p_diag, axis=-1, keepdims=True)
                if i:
                    total = total + jnp.sum(weight, axis=-1, keepdims=True)
                inverse = 1.0 / total
                part = dotf((p_diag * inverse).astype(BF), val[at])
                if i:
                    part = part + dotf((weight * inverse).astype(BF), val[: i * BLOCK])
                result = part if result is None else result + part
                head = 2 * j + side
                lse_ref[at, head : head + 1] = top + jnp.log(total)
            out_ref[at, j * 128 : (j + 1) * 128] = result.astype(BF)


def attend(qkv, tables):
    tokens, width = qkv.shape
    width = width - 2 * HD
    return pl.pallas_call(
        attend_kernel,
        out_shape=(
            jax.ShapeDtypeStruct((tokens, width), BF),
            jax.ShapeDtypeStruct((tokens, 2 * HD), BF),
            jax.ShapeDtypeStruct((tokens, width), BF),
            jax.ShapeDtypeStruct((tokens, width // HD), F32),
        ),
        name="attend",
    )(qkv, *tables)


def attend_back_kernel(
    q_ref, kv_ref, out_ref, grad_ref, lse_ref, cos_ref, sin_ref, cos_kv_ref, sin_kv_ref, d_ref, dk_ref, dv_ref
):
    tokens, width = out_ref.shape
    scale = HD ** (-0.5)
    tiles = width // 128
    keys, vals = padded(kv_ref[...].astype(F32))
    keys = [k.astype(BF) for k in keys]
    vals = [v.astype(BF) for v in vals]
    row = lax.broadcasted_iota(jnp.int32, (BLOCK, BLOCK), 0)
    col = lax.broadcasted_iota(jnp.int32, (BLOCK, BLOCK), 1)
    causal = col <= row
    low = lax.broadcasted_iota(jnp.int32, (BLOCK, 128), 1) < HD
    dk_ref[...] = jnp.zeros_like(dk_ref)
    dv_ref[...] = jnp.zeros_like(dv_ref)
    for i in range(tokens // BLOCK):
        at = slice(i * BLOCK, (i + 1) * BLOCK)
        for j in range(tiles):
            lanes = slice(j * 128, (j + 1) * 128)
            queries = q_ref[at, lanes]
            grads = grad_ref[at, lanes]
            product = grads.astype(F32) * out_ref[at, lanes].astype(F32)
            d_query = None
            for side in range(2):
                key, val = keys[side], vals[side]
                head = 2 * j + side
                lse = lse_ref[at, head : head + 1]
                mine = low if side == 0 else jnp.logical_not(low)
                delta = jnp.sum(jnp.where(mine, product, 0.0), axis=-1, keepdims=True)
                spans = [(at, True)]
                if i:
                    spans.append((slice(0, i * BLOCK), False))
                for span, masked in spans:
                    scores = dot_t(queries, key[span]) * scale
                    if masked:
                        scores = jnp.where(causal, scores, NEG)
                    probs = jnp.exp(scores - lse)
                    d_probs = dot_t(grads, val[span])
                    d_scores = (probs * (d_probs - delta) * scale).astype(BF)
                    dv_ref[side, span] += dot_0(probs.astype(BF), grads)
                    dk_ref[side, span] += dot_0(d_scores, queries)
                    part = dotf(d_scores, key[span])
                    d_query = part if d_query is None else d_query + part
            turned = d_query * cos_ref[at] - halves_swapped(d_query) * sin_ref[at]
            d_ref[at, lanes] = turned.astype(BF)
    full = lax.broadcasted_iota(jnp.int32, (tokens, 128), 1) < HD
    d_key = dk_ref[0] + pltpu.roll(dk_ref[1], HD, 1)
    d_val = dv_ref[1] + pltpu.roll(dv_ref[0], HD, 1)
    tile = jnp.where(full, d_key, d_val)
    turned = tile * cos_kv_ref[...] - halves_swapped(tile) * sin_kv_ref[...]
    d_ref[:, width : width + 128] = turned.astype(BF)


def attend_back(queries, kv, out, grads, lse, tables):
    tokens, width = queries.shape
    return pl.pallas_call(
        attend_back_kernel,
        out_shape=jax.ShapeDtypeStruct((tokens, width + 2 * HD), BF),
        scratch_shapes=[pltpu.VMEM((2, tokens, 128), F32), pltpu.VMEM((2, tokens, 128), F32)],
        name="attend_back",
    )(queries, kv, out, grads, lse, *tables)


def rotary_tables(tokens):
    inverse = BASE ** (-(jnp.arange(HD // 2, dtype=F32) * 2.0) / HD)
    angle = jnp.arange(tokens, dtype=jnp.int32).astype(F32)[:, None] * inverse[None, :]
    cosine, sine = jnp.cos(angle), jnp.sin(angle)
    one, zero = jnp.ones((tokens, HD), F32), jnp.zeros((tokens, HD), F32)
    head_cos = jnp.concatenate([cosine, cosine], axis=1)
    head_sin = jnp.concatenate([-sine, sine], axis=1)
    return (
        jnp.concatenate([head_cos, head_cos], axis=1),
        jnp.concatenate([head_sin, head_sin], axis=1),
        jnp.concatenate([head_cos, one], axis=1),
        jnp.concatenate([head_sin, zero], axis=1),
    )


def inverse_rms(rows):
    return lax.rsqrt(jnp.mean(rows * rows, axis=-1, keepdims=True) + EPS)


def norm_backward(rows, scale, gain, grad):
    weighted = grad * gain
    d_rows = scale * weighted - rows * scale**3 * jnp.mean(weighted * rows, axis=-1, keepdims=True)
    return (d_rows, jnp.sum(grad * rows * scale, axis=0))


def body(
    block_input, cotangent, w_query, w_key, w_value, w_output, w_gate, w_up, w_down, attn_gain, ffn_gain
):
    core = lax.axis_index("ctx")
    place = lax.axis_index("tp")
    slot = lax.axis_index("fsdp")
    count = lax.axis_size("tp")
    both = ("fsdp", "ctx")
    rows = block_input[0]
    cot = cotangent[0]
    local, width = rows.shape
    shard = w_query.shape[0]
    other = 1 - core

    gains = jnp.concatenate([attn_gain, ffn_gain])
    narrow = (w_query.shape[1] + 2 * w_key.shape[1]) // 2
    lines = -(-gains.shape[0] // (16 * narrow)) * 16
    gain_rows = jnp.pad(gains, (0, lines * narrow - gains.shape[0])).reshape(lines, narrow)

    def packed(which):
        return jnp.concatenate(
            [
                jnp.concatenate([half_of(w, which, 1) for w in (w_query, w_key, w_value)], axis=1),
                gain_rows,
            ],
            axis=0,
        )

    qkv_mine = packed(core)
    qkv_theirs = swap(packed(other))
    qkv_shard = pair(qkv_mine, qkv_theirs, core, 0)
    qkv_all = gather_fsdp(qkv_shard)
    qkv_all = qkv_all.reshape(-1, shard + lines, narrow)
    w_qkv = qkv_all[:, :shard].reshape(-1, narrow)
    gain_all = qkv_all[:, shard:].reshape(-1, lines * narrow)[:, : 2 * shard]
    gain_a = gain_all[:, :shard].reshape(-1).astype(F32)
    gain_f = gain_all[:, shard:].reshape(-1).astype(F32)

    wo = lax.all_gather(w_output, both, axis=1, tiled=True)

    def split_cols(w):
        return pair(half_of(w, core, 1), swap(half_of(w, other, 1)), core, 0)

    wg = lax.all_gather(split_cols(w_gate), "fsdp", axis=0, tiled=True)
    wu = lax.all_gather(split_cols(w_up), "fsdp", axis=0, tiled=True)
    wd_shard = pair(half_of(w_down, core, 0), swap(half_of(w_down, other, 0)), core, 1)
    wd = lax.all_gather(wd_shard, "fsdp", axis=1, tiled=True)

    rows_full = pair(rows, swap(rows), core, 0)
    normed = (rows_full * inverse_rms(rows_full) * gain_a).astype(BF)
    tables = rotary_tables(2 * local)
    qkv = dotf(normed, w_qkv)
    queries, kv, attn, lse = attend(qkv, tables)
    attn_own = pair(half_of(attn, core, 0), swap(half_of(attn, other, 0)), core, 1)
    attn_rot = jnp.concatenate(to_rotated(attn_own, place, count), axis=0)

    piece = local // count

    def pieces_of(value):
        return [value[s * piece : (s + 1) * piece] for s in range(count)]

    mine = place * piece
    rows_piece = lax.dynamic_slice_in_dim(rows, mine, piece, 0)
    cot_piece = lax.dynamic_slice_in_dim(cot, mine, piece, 0)
    scale_a = inverse_rms(rows_piece)

    hidden = rows_piece + scatter_tokens(pieces_of(dotf(attn_rot, wo)))
    scale_f = inverse_rms(hidden)
    hnorm_piece = (hidden * scale_f * gain_f).astype(BF)
    hnorm_own = jnp.concatenate(gather_tokens(hnorm_piece), axis=0)
    hnorm = jnp.concatenate([hnorm_own, swap(hnorm_own)], axis=0)

    cot_own = jnp.concatenate(to_rotated(cot.astype(BF), place, count), axis=0)
    cot_b = jnp.concatenate([cot_own, swap(cot_own)], axis=0)

    gate = dotf(hnorm, wg)
    up = dotf(hnorm, wu)
    sigma = jax.nn.sigmoid(gate)
    active = gate * sigma
    inner = (active * up).astype(BF)
    d_inner = dot_t(cot_b, wd)
    d_gate = (d_inner * up * sigma * (1.0 + gate * (1.0 - sigma))).astype(BF)
    d_up = (d_inner * active).astype(BF)

    def over_cores(value):
        return value[:local] + swap(value[local:].astype(BF)).astype(F32)

    d_hnorm = scatter_tokens(pieces_of(over_cores(dot_t(d_gate, wg) + dot_t(d_up, wu))))
    d_norm, g_ffn = norm_backward(hidden, scale_f, gain_f, d_hnorm)
    d_hidden = cot_piece + d_norm
    dh_piece = d_hidden.astype(BF)
    dh_own = jnp.concatenate(gather_tokens(dh_piece), axis=0)

    down = over_cores(dotf(inner, wd))
    out_piece = hidden + scatter_tokens(pieces_of(down))
    out = from_rotated(gather_tokens(out_piece.astype(BF)), place).astype(F32)

    def give_cols(grad):
        other_cols = swap(half_of(grad, other, 0))
        return pair(half_of(grad, core, 0), other_cols, core, 1).astype(F32)

    def reduced(grad, axis):
        return lax.psum_scatter(grad.astype(BF), "fsdp", scatter_dimension=axis, tiled=True)

    part = reduced(dot_0(inner, cot_b), 1)
    s_down = pair(half_of(part, core, 1), swap(half_of(part, other, 1)), core, 0).astype(F32)
    s_gate = give_cols(reduced(dot_0(hnorm, d_gate), 0))
    s_up = give_cols(reduced(dot_0(hnorm, d_up), 0))

    s_output = lax.psum_scatter(
        dot_0(attn_rot, dh_own).astype(BF), both, scatter_dimension=1, tiled=True
    ).astype(F32)
    d_attn_own = from_rotated(pieces_of(dot_t(dh_own, wo).astype(BF)), place)
    d_attn = pair(half_of(d_attn_own, core, 1), swap(half_of(d_attn_own, other, 1)), core, 0)
    d_qkv = attend_back(queries, kv, attn, d_attn, lse, tables)

    d_qkv_rot = jnp.concatenate(
        to_rotated(half_of(d_qkv, core, 0), place, count)
        + to_rotated(half_of(d_qkv, other, 0), place, count),
        axis=0,
    )
    d_normed = scatter_tokens(pieces_of(over_cores(dot_t(d_qkv_rot, w_qkv))))
    d_rows, g_attn = norm_backward(rows_piece, scale_a, gain_a, d_normed)
    d_input = from_rotated(gather_tokens((d_hidden + d_rows).astype(BF)), place).astype(F32)

    part = reduced(dot_0(normed, d_qkv), 0)
    got = swap(half_of(part, other, 0))
    kept = half_of(part, core, 0)
    bounds = [0, w_query.shape[1] // 2, (w_query.shape[1] + w_key.shape[1]) // 2, narrow]
    s_query, s_key, s_value = [
        pair(kept[:, a:b], got[:, a:b], core, 1).astype(F32) for a, b in zip(bounds, bounds[1:])
    ]

    g_all = sum_everywhere(jnp.stack([g_attn, g_ffn]))
    start = (slot * 2 + core) * shard
    s_attn = lax.dynamic_slice_in_dim(g_all[0], start, shard, 0)
    s_ffn = lax.dynamic_slice_in_dim(g_all[1], start, shard, 0)
    return (
        out[None],
        d_input[None],
        s_query,
        s_key,
        s_value,
        s_output,
        s_gate,
        s_up,
        s_down,
        s_attn,
        s_ffn,
    )


def solution(mesh):
    placed = (
        P("fsdp", "ctx", None),
        P("fsdp", "ctx", None),
        P(("fsdp", "ctx"), "tp"),
        P(("fsdp", "ctx"), "tp"),
        P(("fsdp", "ctx"), "tp"),
        P("tp", ("fsdp", "ctx")),
        P(("fsdp", "ctx"), "tp"),
        P(("fsdp", "ctx"), "tp"),
        P("tp", ("fsdp", "ctx")),
        P(("fsdp", "ctx")),
        P(("fsdp", "ctx")),
    )
    return jax.shard_map(
        body,
        mesh=mesh,
        in_specs=placed,
        out_specs=(
            P("fsdp", "ctx", None),
            P("fsdp", "ctx", None),
            P(("fsdp", "ctx"), "tp"),
            P(("fsdp", "ctx"), "tp"),
            P(("fsdp", "ctx"), "tp"),
            P("tp", ("fsdp", "ctx")),
            P(("fsdp", "ctx"), "tp"),
            P(("fsdp", "ctx"), "tp"),
            P("tp", ("fsdp", "ctx")),
            P(("fsdp", "ctx")),
            P(("fsdp", "ctx")),
        ),
        check_vma=False,
    )
```

```python
import jax
import jax.numpy as jnp
from jax import lax
from jax.experimental import pallas as pl
from jax.experimental.pallas import tpu as pltpu
from jax.sharding import PartitionSpec as P

HD = 64
EPS = 1e-05
BASE = 500000.0
NEG = -1e30
BF = jnp.bfloat16
F32 = jnp.float32
BLOCK = 256


def dotf(left, right):
    return jnp.dot(left, right, preferred_element_type=F32)


def dot_t(left, right):
    return lax.dot_general(left, right, (((1,), (1,)), ((), ())), preferred_element_type=F32)


def dot_0(left, right):
    return lax.dot_general(left, right, (((0,), (0,)), ((), ())), preferred_element_type=F32)


def after(value, *others):
    return lax.optimization_barrier((value,) + others)[0]


def swap(value):
    return lax.ppermute(value, "ctx", [(0, 1), (1, 0)])


def pair(mine, theirs, core, axis):
    first = jnp.where(core == 0, mine, theirs)
    second = jnp.where(core == 0, theirs, mine)
    return jnp.concatenate([first, second], axis=axis)


def half_of(value, which, axis):
    size = value.shape[axis] // 2
    return lax.dynamic_slice_in_dim(value, which * size, size, axis)


def xor_pairs(axis, bit):
    return [(k, k ^ bit) for k in range(lax.axis_size(axis))]


def bits_of(axis):
    return [1 << b for b in range(lax.axis_size(axis).bit_length() - 1)]


def gated(value, gate):
    return value if gate is None else after(value, gate)


def near_far():
    return xor_pairs("tp", 1), xor_pairs("tp", 2)


def halved(values, pairs):
    half = values[0].shape[0] // 2
    sent = jnp.concatenate([v[half:].astype(BF) for v in values], axis=0)
    return [v[:half] for v in values], lax.ppermute(sent, "tp", pairs)


def summed(kept, got):
    half = kept[0].shape[0]
    return [
        k.astype(F32) + got[n * half : (n + 1) * half].astype(F32) for n, k in enumerate(kept)
    ]


def position(index, place, count):
    distance = index ^ place
    result = distance & 0
    for bit in range(count.bit_length() - 1):
        result = result * 2 + ((distance >> bit) & 1)
    return result


def arrange(parts, place_at, kind, back):
    count = lax.axis_size("tp")
    rows = parts[0].shape[0]
    size = rows // count
    width = parts[0].shape[1]
    columns = width // 4

    def kernel(place_ref, *refs):
        out_ref = refs[-1]
        for n in range(len(parts)):
            for j in range(count):
                natural = slice(j * size, (j + 1) * size)
                at = pl.multiple_of(position(j, place_ref[0], count) * size, size)
                if back:
                    out_ref[n * rows + j * size : n * rows + (j + 1) * size, :] = refs[n][
                        pl.ds(at, size), :
                    ].astype(kind)
                else:
                    to = pl.ds(pl.multiple_of(n * rows + at, size), size)
                    out_ref[to, :] = refs[n][natural, :].astype(kind)

    return pl.pallas_call(
        kernel,
        grid_spec=pltpu.PrefetchScalarGridSpec(
            num_scalar_prefetch=1,
            grid=(4,),
            in_specs=[pl.BlockSpec((rows, columns), lambda i, at: (0, i)) for _ in parts],
            out_specs=pl.BlockSpec((rows * len(parts), columns), lambda i, at: (0, i)),
        ),
        out_shape=jax.ShapeDtypeStruct((rows * len(parts), width), kind),
        name="arrange",
    )(place_at, *parts)


class Scatter:
    def __init__(self, grad):
        self.plain = grad.shape[0] != 4
        if self.plain:
            self.whole = lax.psum_scatter(grad, "fsdp", scatter_dimension=0, tiled=False)
            return
        me = lax.axis_index("fsdp")
        cut = grad.shape[1] // 32 * 16
        self.near, self.far = xor_pairs("fsdp", 1), xor_pairs("fsdp", 2)
        self.top, self.low = slice(0, cut), slice(cut, None)
        self.blocks = [lax.dynamic_index_in_dim(grad, me ^ k, 0, keepdims=False) for k in range(4)]
        one, two, three = self.blocks[1:]
        self.by_near = lax.ppermute(jnp.stack([one[self.top], three[self.top]]), "fsdp", self.near)
        self.by_far = lax.ppermute(jnp.stack([two[self.low], three[self.low]]), "fsdp", self.far)

    def second(self, *gate):
        if self.plain:
            self.token = self.whole
            return
        by_near, by_far = lax.optimization_barrier((self.by_near, self.by_far) + gate)[:2]
        own, one, two = [b.astype(F32) for b in self.blocks[:3]]
        self.a_own = own[self.top] + by_near[0].astype(F32)
        self.b_own = own[self.low] + by_far[0].astype(F32)
        a_far = (two[self.top] + by_near[1].astype(F32)).astype(BF)
        b_near = (one[self.low] + by_far[1].astype(F32)).astype(BF)
        self.token = b_near
        self.a_got = lax.ppermute(a_far, "fsdp", self.far)
        self.b_got = lax.ppermute(b_near, "fsdp", self.near)

    def third(self, *gate):
        if self.plain:
            return self.whole
        a, b = lax.optimization_barrier((self.a_got, self.b_got) + gate)[:2]
        return jnp.concatenate(
            [(self.a_own + a.astype(F32)).astype(BF), (self.b_own + b.astype(F32)).astype(BF)], axis=0
        )


class Gather:
    def __init__(self, shard, axis=0):
        self.shard, self.axis, self.plain = shard, axis, lax.axis_size("fsdp") != 4

    def first(self, *gate):
        shard = after(self.shard, *gate) if gate else self.shard
        if self.plain:
            self.whole = lax.all_gather(shard, "fsdp", axis=self.axis, tiled=True)
            return self.whole
        self.one = lax.ppermute(shard, "fsdp", xor_pairs("fsdp", 1))
        self.two = lax.ppermute(shard, "fsdp", xor_pairs("fsdp", 2))
        return self.two

    def second(self, *gate):
        if self.plain:
            return self.whole
        one, two = self.one, self.two
        if gate:
            one, two = lax.optimization_barrier((one, two) + gate)[:2]
        cut = self.shard.shape[0] // 32 * 16
        far = lax.ppermute(one[:cut], "fsdp", xor_pairs("fsdp", 2))
        near = lax.ppermute(two[cut:], "fsdp", xor_pairs("fsdp", 1))
        return [self.shard, one, two, jnp.concatenate([far, near], axis=0)]


def in_order(pieces, axis, rows=slice(None)):
    if not isinstance(pieces, list):
        count = lax.axis_size("fsdp")
        size = pieces.shape[axis] // count
        pieces = [lax.slice_in_dim(pieces, k * size, (k + 1) * size, axis=axis)[rows] for k in range(count)]
        return jnp.concatenate(pieces, axis=axis)
    me = lax.axis_index("fsdp")
    low, high = (me & 1) == 0, (me & 2) == 0
    own, one, two, three = [p[rows] for p in pieces]
    a, b = jnp.where(low, own, one), jnp.where(low, one, own)
    c, d = jnp.where(low, two, three), jnp.where(low, three, two)
    return jnp.concatenate(
        [jnp.where(high, a, c), jnp.where(high, b, d), jnp.where(high, c, a), jnp.where(high, d, b)],
        axis=axis,
    )


def sum_steps(value, steps):
    for axis, bit in steps:
        value = value + lax.ppermute(value, axis, xor_pairs(axis, bit))
    return value


def grad_kernel(lefts, rights, column, columns, block):
    rows, wide = lefts[0].shape

    def kernel(*refs):
        total = dot_0(refs[0][...], refs[len(lefts)][...])
        for n in range(1, len(lefts)):
            total = total + dot_0(refs[n][...], refs[len(lefts) + n][...])
        refs[-1][...] = total.astype(BF)

    return pl.pallas_call(
        kernel,
        grid=(wide // block,),
        in_specs=[pl.BlockSpec((rows, block), lambda i: (0, i)) for _ in lefts]
        + [pl.BlockSpec((rows, columns), lambda i: (0, column)) for _ in rights],
        out_specs=pl.BlockSpec((block, columns), lambda i: (i, 0)),
        out_shape=jax.ShapeDtypeStruct((wide, columns), BF),
        name="grad",
    )(*lefts, *rights)


def halves_swapped(tile):
    lane = lax.broadcasted_iota(jnp.int32, tile.shape, 1)
    width = tile.shape[1]
    back = pltpu.roll(tile, width - HD // 2, 1)
    ahead = pltpu.roll(tile, HD // 2, 1)
    return jnp.where(lane % HD < HD // 2, back, ahead)


def padded(kv):
    lane = lax.broadcasted_iota(jnp.int32, kv.shape, 1)
    low = lane < HD
    other = pltpu.roll(kv, HD, 1)
    zero = jnp.zeros_like(kv)
    keys = (jnp.where(low, kv, zero), jnp.where(low, zero, other))
    vals = (jnp.where(low, other, zero), jnp.where(low, zero, kv))
    return [k.astype(BF) for k in keys], [v.astype(BF) for v in vals]


def causal_mask():
    row = lax.broadcasted_iota(jnp.int32, (BLOCK, BLOCK), 0)
    col = lax.broadcasted_iota(jnp.int32, (BLOCK, BLOCK), 1)
    return col <= row


def spread(ref, base, place, count, lanes, value):
    size = value.shape[0] // count
    for j in range(count):
        at = pl.multiple_of(base + position(j, place, count) * size, size)
        ref[pl.ds(at, size), lanes] = value[j * size : (j + 1) * size]


def collect(ref, base, place, count, lanes, rows):
    size = rows // count
    return jnp.concatenate(
        [
            ref[pl.ds(pl.multiple_of(base + position(j, place, count) * size, size), size), lanes]
            for j in range(count)
        ],
        axis=0,
    )


def attend_blocks(at_ref, q_ref, keys, vals, out_ref, lse_ref, blocks, count):
    core, place = at_ref[0], at_ref[1]
    width = out_ref.shape[1]
    scale = HD ** (-0.5)
    causal = causal_mask()
    for n, i in enumerate(blocks):
        at = slice(i * BLOCK, (i + 1) * BLOCK)
        to = slice(n * BLOCK, (n + 1) * BLOCK)
        for j in range(width // 128):
            lanes = slice(j * 128, (j + 1) * 128)
            queries = q_ref[at, lanes]
            result = None
            for side in range(2):
                key, val = keys[side], vals[side]
                diag = dot_t(queries, key[at]) * scale
                diag = jnp.where(causal, diag, NEG)
                top = jnp.max(diag, axis=-1, keepdims=True)
                if i:
                    past = dot_t(queries, key[: i * BLOCK]) * scale
                    top = jnp.maximum(top, jnp.max(past, axis=-1, keepdims=True))
                    weight = jnp.exp(past - top)
                p_diag = jnp.exp(diag - top)
                total = jnp.sum(p_diag, axis=-1, keepdims=True)
                if i:
                    total = total + jnp.sum(weight, axis=-1, keepdims=True)
                inverse = 1.0 / total
                part = dotf(p_diag.astype(BF), val[at])
                if i:
                    part = part + dotf(weight.astype(BF), val[: i * BLOCK])
                part = part * inverse
                result = part if result is None else result + part
                head = 2 * j + side
                lse_ref[to, head : head + 1] = top + jnp.log(total)
            spread(out_ref, (core ^ n) * BLOCK, place, count, lanes, result.astype(BF))


SCALARS = pl.BlockSpec(memory_space=pltpu.SMEM)


def attend_first(at, qkv, tables, blocks, count):
    tokens, width = qkv.shape
    width = width - 2 * HD
    local = tokens // 2

    def kernel(at_ref, qkv_ref, cos_ref, sin_ref, cos_kv_ref, sin_kv_ref, q_ref, kv_ref, out_ref, lse_ref):
        core = at_ref[0]
        for half in range(2):
            to = slice(half * local, (half + 1) * local)
            source = pl.ds(pl.multiple_of((core ^ half) * local, local), local)
            for j in range(width // 128):
                tile = qkv_ref[source, j * 128 : (j + 1) * 128]
                turned = tile * cos_ref[to] + halves_swapped(tile) * sin_ref[to]
                q_ref[to, j * 128 : (j + 1) * 128] = turned.astype(BF)
            tile = qkv_ref[source, width : width + 128]
            turned = tile * cos_kv_ref[to] + halves_swapped(tile) * sin_kv_ref[to]
            kv_ref[to, :] = turned.astype(BF)
        keys, vals = padded(kv_ref[...].astype(F32))
        attend_blocks(at_ref, q_ref, keys, vals, out_ref, lse_ref, blocks, count)

    rows = len(blocks) * BLOCK
    return pl.pallas_call(
        kernel,
        in_specs=[SCALARS] + [pl.BlockSpec()] * 5,
        out_shape=(
            jax.ShapeDtypeStruct((tokens, width), BF),
            jax.ShapeDtypeStruct((tokens, 2 * HD), BF),
            jax.ShapeDtypeStruct((rows, width), BF),
            jax.ShapeDtypeStruct((rows, width // HD), F32),
        ),
        name="attend_first",
    )(at, qkv, *tables)


def attend_next(at, queries, kv, blocks, count):
    width = queries.shape[1]

    def kernel(at_ref, q_ref, kv_ref, out_ref, lse_ref):
        keys, vals = padded(kv_ref[...].astype(F32))
        attend_blocks(at_ref, q_ref, keys, vals, out_ref, lse_ref, blocks, count)

    rows = len(blocks) * BLOCK
    return pl.pallas_call(
        kernel,
        in_specs=[SCALARS] + [pl.BlockSpec()] * 2,
        out_shape=(
            jax.ShapeDtypeStruct((rows, width), BF),
            jax.ShapeDtypeStruct((rows, width // HD), F32),
        ),
        name="attend_next",
    )(at, queries, kv)


def attend_back(at, queries, kv, out, grads, lse, tables, blocks, carried, count):
    tokens, width = queries.shape
    scale = HD ** (-0.5)
    tiles = width // 128
    last = carried is not None

    def kernel(at_ref, q_ref, kv_ref, out_ref, mine_ref, theirs_ref, lse_ref, cos_ref, sin_ref, cos_kv_ref, sin_kv_ref, *refs):
        if last:
            dk_in, dv_in, dq_ref, dq_to_ref, dkv_ref, dkv_to_ref, dk_ref, dv_ref = refs
        else:
            dq_ref, dq_to_ref, dk_ref, dv_ref = refs
        core, place = at_ref[0], at_ref[1]
        keys, vals = padded(kv_ref[...].astype(F32))
        causal = causal_mask()
        low = lax.broadcasted_iota(jnp.int32, (BLOCK, 128), 1) < HD
        if last:
            dk_ref[...] = dk_in[...]
            dv_ref[...] = dv_in[...]
        else:
            dk_ref[...] = jnp.zeros_like(dk_ref)
            dv_ref[...] = jnp.zeros_like(dv_ref)
        for n, i in enumerate(blocks):
            at = slice(i * BLOCK, (i + 1) * BLOCK)
            to = slice(n * BLOCK, (n + 1) * BLOCK)
            for j in range(tiles):
                lanes = slice(j * 128, (j + 1) * 128)
                query = q_ref[at, lanes]
                mine = collect(mine_ref, 0, place, count, lanes, BLOCK).astype(F32)
                theirs = collect(theirs_ref, 0, place, count, lanes, BLOCK).astype(F32)
                grad_f = jnp.where(core == n, mine, theirs)
                grad = grad_f.astype(BF)
                result = collect(out_ref, (core ^ n) * BLOCK, place, count, lanes, BLOCK)
                product = grad_f * result.astype(F32)
                d_query = None
                for side in range(2):
                    key, val = keys[side], vals[side]
                    head = 2 * j + side
                    top = lse_ref[to, head : head + 1]
                    part_of = low if side == 0 else jnp.logical_not(low)
                    delta = jnp.sum(jnp.where(part_of, product, 0.0), axis=-1, keepdims=True)
                    spans = [(at, True)]
                    if i:
                        spans.append((slice(0, i * BLOCK), False))
                    for span, masked in spans:
                        scores = dot_t(query, key[span]) * scale
                        if masked:
                            scores = jnp.where(causal, scores, NEG)
                        probs = jnp.exp(scores - top)
                        d_probs = dot_t(grad, val[span])
                        d_scores = (probs * (d_probs - delta) * scale).astype(BF)
                        dv_ref[side, span] += dot_0(probs.astype(BF), grad)
                        dk_ref[side, span] += dot_0(d_scores, query)
                        part = dotf(d_scores, key[span])
                        d_query = part if d_query is None else d_query + part
                turned = d_query * cos_ref[at] - halves_swapped(d_query) * sin_ref[at]
                turned = turned.astype(BF)
                dq_ref[pl.ds(pl.multiple_of((core ^ n) * BLOCK, BLOCK), BLOCK), lanes] = turned
                spread(dq_to_ref, (core ^ n) * BLOCK, place, count, lanes, turned)
        if last:
            full = lax.broadcasted_iota(jnp.int32, (tokens, 128), 1) < HD
            d_key = dk_ref[0] + pltpu.roll(dk_ref[1], HD, 1)
            d_val = dv_ref[1] + pltpu.roll(dv_ref[0], HD, 1)
            tile = jnp.where(full, d_key, d_val)
            turned = tile * cos_kv_ref[...] - halves_swapped(tile) * sin_kv_ref[...]
            turned = turned.astype(BF)
            half = tokens // 2
            for c in range(2):
                base = (core ^ c) * half
                dkv_ref[pl.ds(pl.multiple_of(base, half), half), :] = turned[c * half : (c + 1) * half]
                for i in range(half // BLOCK):
                    rows = turned[c * half + i * BLOCK : c * half + (i + 1) * BLOCK]
                    spread(dkv_to_ref, base + i * BLOCK, place, count, slice(0, 128), rows)

    sums = [((2, tokens, 128), F32)] * 2
    rows = len(blocks) * BLOCK
    shapes = [jax.ShapeDtypeStruct((rows, width), BF)] * 2
    if last:
        shapes += [jax.ShapeDtypeStruct((tokens, 2 * HD), BF)] * 2
    else:
        shapes += [jax.ShapeDtypeStruct(*s) for s in sums]
    return pl.pallas_call(
        kernel,
        in_specs=[SCALARS] + [pl.BlockSpec()] * (10 + 2 * last),
        out_shape=tuple(shapes),
        scratch_shapes=[pltpu.VMEM(*s) for s in sums] if last else [],
        name="attend_back",
    )(at, queries, kv, out, *grads, lse, *tables, *(carried or ()))


def rotary_tables(tokens):
    lane = lax.broadcasted_iota(jnp.int32, (1, 2 * HD), 1)
    inverse = BASE ** (-((lane % (HD // 2)).astype(F32) * 2.0) / HD)
    angle = lax.broadcasted_iota(jnp.int32, (tokens, 2 * HD), 0).astype(F32) * inverse
    cosine, sine = jnp.cos(angle), jnp.sin(angle) * jnp.where(lane % HD < HD // 2, -1.0, 1.0)
    keyed = lane < HD
    return (cosine, sine, jnp.where(keyed, cosine, 1.0), jnp.where(keyed, sine, 0.0))


def inverse_rms(rows):
    return lax.rsqrt(jnp.mean(rows * rows, axis=-1, keepdims=True) + EPS)


def norm_backward(rows, scale, gain, grad):
    weighted = grad * gain
    d_rows = scale * weighted - rows * scale**3 * jnp.mean(weighted * rows, axis=-1, keepdims=True)
    return (d_rows, jnp.sum(grad * rows * scale, axis=0))


def stack(*parts):
    return jnp.concatenate(parts, axis=0)


CHUNKS = 2


def body(
    block_input, cotangent, w_query, w_key, w_value, w_output, w_gate, w_up, w_down, attn_gain, ffn_gain
):
    core = lax.axis_index("ctx")
    place = lax.axis_index("tp")
    slot = lax.axis_index("fsdp")
    count = lax.axis_size("tp")
    fsdp = lax.axis_size("fsdp")
    near, far = near_far()
    rows = block_input[0]
    cot = cotangent[0]
    local, width = rows.shape
    shard = w_query.shape[0]
    other = 1 - core
    span = local // CHUNKS
    piece = span // count
    units = w_gate.shape[1] // 2
    where = jnp.stack([core, place]).astype(jnp.int32)
    place_at = place.astype(jnp.int32).reshape(1)

    gains = jnp.concatenate([attn_gain, ffn_gain])
    narrow = (w_query.shape[1] + 2 * w_key.shape[1]) // 2
    lines = -(-gains.shape[0] // (16 * narrow)) * 16
    gain_rows = jnp.pad(gains, (0, lines * narrow - gains.shape[0])).reshape(lines, narrow)

    def packed(which):
        halves = [half_of(w, which, 1) for w in (w_query, w_key, w_value)]
        return stack(jnp.concatenate(halves, axis=1), gain_rows)

    def packed_gu(which):
        return jnp.concatenate([half_of(w_gate, which, 1), half_of(w_up, which, 1)], axis=1)

    qkv_mine, qkv_got = packed(core), swap(packed(other))
    gu_got = swap(after(packed_gu(other), qkv_got))
    rows_theirs = swap(after(rows, qkv_got))
    wd_got = swap(after(half_of(w_down, other, 0), rows_theirs))
    get_qkv = Gather(
        stack(
            pair(qkv_mine[:shard], qkv_got[:shard], core, 0), pair(qkv_mine[shard:], qkv_got[shard:], core, 0)
        )
    )
    get_wo = Gather(w_output, 1)
    t_qkv = get_qkv.first()
    w_gu = lax.all_gather(pair(packed_gu(core), gu_got, core, 0), "fsdp", axis=0, tiled=True)
    wd = lax.all_gather(
        pair(half_of(w_down, core, 0), wd_got, core, 1), "fsdp", axis=1, tiled=True
    )
    scale_own, scale_theirs = inverse_rms(rows), inverse_rms(rows_theirs)
    tables = rotary_tables(2 * local)
    qkv_pieces = get_qkv.second(scale_own)
    t_wo = get_wo.first(t_qkv)
    w_qkv = in_order(qkv_pieces, 0, slice(0, 2 * shard))
    gain_all = in_order(qkv_pieces, 0, slice(2 * shard, None)).reshape(-1, lines * narrow)
    w_qkv, gain_all = lax.optimization_barrier((w_qkv, gain_all, scale_theirs) + tuple(tables))[:2]
    gain_a = gain_all[:, :shard].reshape(-1).astype(F32)
    gain_f = gain_all[:, shard : 2 * shard].reshape(-1).astype(F32)

    normed = stack(
        (rows * scale_own * gain_a).astype(BF), (rows_theirs * scale_theirs * gain_a).astype(BF)
    )
    qkv = dotf(normed, w_qkv)
    blocks = [[h * span // BLOCK, h * span // BLOCK + local // BLOCK] for h in range(CHUNKS)]
    queries, kv, attn_0, lse_0 = attend_first(where, qkv, tables, blocks[0], count)

    wo_mine = in_order(get_wo.second(qkv), 1)
    wo_theirs = swap(wo_mine)
    wo_halves = [w.reshape(w.shape[0], -1, shard) for w in (wo_mine, wo_theirs)]
    first = jnp.where(core == 0, wo_halves[0], wo_halves[1])
    second = jnp.where(core == 0, wo_halves[1], wo_halves[0])
    wo = jnp.stack([first, second], axis=2).reshape(w_output.shape[0], width)
    wo_a, wo_b = lax.optimization_barrier((half_of(wo, core, 0), half_of(wo, other, 0)))

    def slice_of(value, h):
        return lax.dynamic_slice_in_dim(value, h * span + place * piece, piece, 0)

    attn_1, lse_1 = attend_next(where, queries, kv, blocks[1], count)
    attn, lse = [attn_0, attn_1], [lse_0, lse_1]
    attn_own = [(a[:span], swap(a[span:])) for a in attn]
    partial = [dotf(mine, wo_a) + dotf(theirs, wo_b) for mine, theirs in attn_own]

    def hidden_of(h, total):
        hidden = slice_of(rows, h) + total
        scale = inverse_rms(hidden)
        return hidden, scale, (hidden * scale * gain_f).astype(BF)

    k0, g0 = halved([partial[0]], near)
    k1, g1 = halved([partial[1]], near)
    v0 = summed(k0, after(g0, partial[1]))
    k0, g0 = halved(v0, far)
    v1 = summed(k1, after(g1, v0[0]))
    k1, g1 = halved(v1, far)
    hidden_0, scale_0, c0 = hidden_of(0, summed(k0, after(g0, v1[0]))[0])
    a0 = lax.ppermute(c0, "tp", far)
    hidden_1, scale_1, c1 = hidden_of(1, summed(k1, after(g1, c0))[0])
    a1 = lax.ppermute(c1, "tp", far)
    cur0 = stack(c0, after(a0, c1))
    b0, s0 = lax.ppermute(cur0, "tp", near), swap(cur0)
    cur1 = stack(c1, after(a1, cur0))
    b1, s1 = lax.ppermute(cur1, "tp", near), swap(cur1)

    cot_gated = after(cot.astype(BF), v1[0])
    cot_own = arrange([cot_gated[h * span : (h + 1) * span] for h in range(CHUNKS)], place_at, BF, False)
    cot_theirs = swap(cot_own)
    cots = [
        stack(cot_own[h * span : (h + 1) * span], cot_theirs[h * span : (h + 1) * span])
        for h in range(CHUNKS)
    ]

    def backward_of(gu, d_inner):
        gate, up = gu[:, :units], gu[:, units:]
        sigma = jax.nn.sigmoid(gate)
        active = gate * sigma
        d_gate = (d_inner * up * sigma * (1.0 + gate * (1.0 - sigma))).astype(BF)
        d_up = (d_inner * active).astype(BF)
        return (active * up).astype(BF), jnp.concatenate([d_gate, d_up], axis=1)

    b0 = after(b0, cur1, *cots)
    hnorm_0 = stack(cur0, b0, s0, swap(b0))
    gu_0 = dotf(hnorm_0, w_gu)
    b1 = after(b1, gu_0)
    s_b1 = swap(b1)
    inner_0, d_gu_0 = backward_of(gu_0, dot_t(cots[0], wd))
    d_full_0 = dot_t(d_gu_0, w_gu)
    s0 = swap(d_full_0[span:].astype(BF))
    cur1, b1, s1, s_b1 = lax.optimization_barrier((cur1, b1, s1, s_b1, d_full_0))[:4]
    hnorm_1 = stack(cur1, b1, s1, s_b1)
    gu_1 = dotf(hnorm_1, w_gu)
    d0 = d_full_0[:span] + after(s0, gu_1).astype(F32)
    k0, g0 = halved([d0], near)
    inner_1, d_gu_1 = backward_of(gu_1, dot_t(after(cots[1], d0), wd))
    d_full_1 = dot_t(d_gu_1, w_gu)
    s1 = swap(d_full_1[span:].astype(BF))
    v0 = summed(k0, after(g0, d_full_1))
    k0, g0 = halved(v0, far)
    d1 = d_full_1[:span] + after(s1, v0[0]).astype(F32)
    k1, g1 = halved([d1], near)

    def reduced(grad, axis):
        return lax.psum_scatter(grad, "fsdp", scatter_dimension=axis, tiled=True)

    def gradient(lefts, rights, column, *gate):
        n = len(rights)
        rights = lax.optimization_barrier(tuple(rights) + gate)[:n]
        return grad_kernel(lefts, rights, column, units if column is not None else width, 512)

    d_gu, inner, hnorm = [d_gu_0, d_gu_1], [inner_0, inner_1], [hnorm_0, hnorm_1]
    g_gate = gradient(hnorm, d_gu, 0, v0[0], d1)

    def back_of(h, hidden, scale, total):
        d_norm, gain = norm_backward(hidden, scale, gain_f, total)
        d_hidden = slice_of(cot, h) + d_norm
        return d_hidden, gain, d_hidden.astype(BF)

    dh_0, gain_0, c0 = back_of(0, hidden_0, scale_0, summed(k0, after(g0, g_gate))[0])
    a0 = lax.ppermute(c0, "tp", far)
    v1 = summed(k1, after(g1, c0))
    k1, g1 = halved(v1, far)
    g_up = gradient(hnorm, d_gu, 1, c0, v1[0])
    cur0 = stack(c0, after(a0, g_up))
    b0 = lax.ppermute(cur0, "tp", near)
    dh_1, gain_1, c1 = back_of(1, hidden_1, scale_1, summed(k1, after(g1, cur0))[0])
    a1 = lax.ppermute(c1, "tp", far)
    g_ffn = gain_0 + gain_1
    g_down = grad_kernel(inner, lax.optimization_barrier(tuple(cots) + (cur0, c1))[:2], 0, width, 512)
    down = [dotf(after(i, g_down), wd) for i in inner]
    s_down = swap(stack(*[d[span:].astype(BF) for d in down]))
    r_gate, r_up, r_down = reduced(g_gate, 0), reduced(g_up, 0), reduced(g_down, 1)
    full_0 = stack(cur0, after(b0, *down))
    cur1 = stack(c1, after(a1, full_0))
    b1 = lax.ppermute(cur1, "tp", near)
    down = [
        d[:span] + after(s_down, cur1)[n * span : (n + 1) * span].astype(F32) for n, d in enumerate(down)
    ]
    k_out, g_out = halved(down, near)

    def grads_of(full):
        send = swap(dot_t(full, wo_b).astype(BF))
        return dot_t(full, wo_a).astype(BF), send

    dq_0, dq_to_0, *carried = attend_back(
        where, queries, kv, attn_0, grads_of(after(full_0, *down)), lse_0, tables, blocks[0], None, count
    )
    v_out = summed(k_out, after(g_out, dq_0))
    k_out, g_out = halved(v_out, far)
    full_1 = stack(cur1, after(b1, *v_out))
    dq_1, dq_to_1, d_kv, d_kv_to = attend_back(
        where, queries, kv, attn_1, grads_of(full_1), lse_1, tables, blocks[1], carried, count
    )

    def joined(query, kv_of, h, side):
        at = side * local + h * span
        return jnp.concatenate([query[side * span : (side + 1) * span], kv_of[at : at + span]], axis=1)

    parts = [
        dot_t(stack(*[joined(q, d_kv_to, h, s) for s in range(2)]), w_qkv)
        for h, q in enumerate((dq_to_0, dq_to_1))
    ]
    sent = [swap(p[span:].astype(BF)) for p in parts]
    d_qkv = stack(*[joined(q, d_kv, h, s) for s in range(2) for h, q in enumerate((dq_0, dq_1))])
    g_qkv = dot_0(normed, after(d_qkv, *parts)).astype(BF)
    d0 = parts[0][:span] + after(sent[0], g_qkv).astype(F32)
    d1 = parts[1][:span] + after(sent[1], g_qkv).astype(F32)
    k0, g0 = halved([d0], near)
    k1, g1 = halved([d1], near)
    totals = summed(k_out, after(g_out, d0, d1))
    c_out = stack(hidden_0 + totals[0], hidden_1 + totals[1]).astype(BF)
    a_out = lax.ppermute(c_out, "tp", far)

    dh_all = after(stack(full_0, full_1), c_out)
    g_mine = dot_0(stack(*[a[0] for a in attn_own]), dh_all).astype(BF)
    g_theirs = dot_0(stack(*[a[1] for a in attn_own]), dh_all).astype(BF)

    def columns(grad, which):
        grad = grad.reshape(grad.shape[0], fsdp, 2, shard)
        return lax.dynamic_index_in_dim(grad, which, 2, keepdims=False)

    got = swap(stack(columns(g_theirs, other), columns(g_mine, other)))
    g_output = stack(columns(g_mine, core), columns(g_theirs, core)).astype(F32) + got.astype(F32)
    g_output = g_output.astype(BF).swapaxes(0, 1)
    g_qkv = g_qkv.reshape(fsdp, -1, narrow)
    joint = g_qkv.shape[1] == g_output.shape[1]
    if joint:
        reduce = [Scatter(jnp.concatenate([g_qkv, g_output], axis=2))]
    else:
        reduce = [Scatter(g_qkv), Scatter(g_output)]

    v0 = summed(k0, after(g0, g_output))
    k0, g0 = halved(v0, far)
    v1 = summed(k1, after(g1, v0[0]))
    k1, g1 = halved(v1, far)
    cur_out = stack(*[stack(c_out[h * piece : (h + 1) * piece], after(a_out, v1[0])[h * piece : (h + 1) * piece]) for h in range(CHUNKS)])
    b_out = lax.ppermute(cur_out, "tp", near)
    for item in reduce:
        item.second(cur_out)

    def input_of(h, d_hidden, total):
        d_rows, gain = norm_backward(slice_of(rows, h), slice_of(scale_own, h), gain_a, total)
        return gain, (d_hidden + d_rows).astype(BF)

    gain_0, c0 = input_of(0, dh_0, summed(k0, after(g0, *[r.token for r in reduce]))[0])
    a0 = lax.ppermute(c0, "tp", far)
    gain_1, c1 = input_of(1, dh_1, summed(k1, after(g1, c0))[0])
    a1 = lax.ppermute(c1, "tp", far)
    g_all = sum_steps(jnp.stack([gain_0 + gain_1, g_ffn]), [("ctx", 1)])
    cur0 = stack(c0, after(a0, c1, g_all))
    b0 = lax.ppermute(cur0, "tp", near)
    cur1 = stack(c1, after(a1, cur0))
    b1 = lax.ppermute(cur1, "tp", near)

    r_down, r_gate, r_up = lax.optimization_barrier((r_down, r_gate, r_up, cur1))[:3]
    s_down = pair(half_of(r_down, core, 1), swap(half_of(r_down, other, 1)), core, 0).astype(F32)
    s_gate = pair(half_of(r_gate, core, 0), swap(half_of(r_gate, other, 0)), core, 1).astype(F32)
    s_up = pair(half_of(r_up, core, 0), swap(half_of(r_up, other, 0)), core, 1).astype(F32)

    half = span
    cur_half, got_half = cur_out.shape[0] // CHUNKS, b_out.shape[0] // CHUNKS
    b_out = after(b_out, cur1)
    out = arrange(
        [
            stack(cur_out[h * cur_half : (h + 1) * cur_half], b_out[h * got_half : (h + 1) * got_half])
            for h in range(CHUNKS)
        ],
        place_at,
        F32,
        True,
    )
    g_all = sum_steps(after(g_all, cur1), [("tp", 1), ("tp", 2)] + [("fsdp", b) for b in bits_of("fsdp")])

    results = [item.third(out) for item in reduce]
    if joint:
        r_qkv, r_output = results[0][:, :narrow], results[0][:, narrow:]
    else:
        r_qkv, r_output = results
    half = r_output.shape[0] // 2
    s_output = pair(r_output[:half], r_output[half:], core, 0).astype(F32)
    mine, theirs = half_of(r_qkv, core, 0), swap(half_of(r_qkv, other, 0))
    bounds = [0, w_query.shape[1] // 2, (w_query.shape[1] + w_key.shape[1]) // 2, narrow]
    s_query, s_key, s_value = [
        pair(mine[:, a:b], theirs[:, a:b], core, 1).astype(F32) for a, b in zip(bounds, bounds[1:])
    ]
    d_input = arrange([stack(cur0, b0), stack(cur1, b1)], place_at, F32, True)

    start = (slot * 2 + core) * shard
    s_attn = lax.dynamic_slice_in_dim(g_all[0], start, shard, 0)
    s_ffn = lax.dynamic_slice_in_dim(g_all[1], start, shard, 0)
    return (
        out[None],
        d_input[None],
        s_query,
        s_key,
        s_value,
        s_output,
        s_gate,
        s_up,
        s_down,
        s_attn,
        s_ffn,
    )


def solution(mesh):
    placed = (
        P("fsdp", "ctx", None),
        P("fsdp", "ctx", None),
        P(("fsdp", "ctx"), "tp"),
        P(("fsdp", "ctx"), "tp"),
        P(("fsdp", "ctx"), "tp"),
        P("tp", ("fsdp", "ctx")),
        P(("fsdp", "ctx"), "tp"),
        P(("fsdp", "ctx"), "tp"),
        P("tp", ("fsdp", "ctx")),
        P(("fsdp", "ctx")),
        P(("fsdp", "ctx")),
    )
    return jax.shard_map(
        body,
        mesh=mesh,
        in_specs=placed,
        out_specs=(
            P("fsdp", "ctx", None),
            P("fsdp", "ctx", None),
            P(("fsdp", "ctx"), "tp"),
            P(("fsdp", "ctx"), "tp"),
            P(("fsdp", "ctx"), "tp"),
            P("tp", ("fsdp", "ctx")),
            P(("fsdp", "ctx"), "tp"),
            P(("fsdp", "ctx"), "tp"),
            P("tp", ("fsdp", "ctx")),
            P(("fsdp", "ctx")),
            P(("fsdp", "ctx")),
        ),
        check_vma=False,
    )
```

```python
import jax
import jax.numpy as jnp
from jax import lax
from jax.experimental import pallas as pl
from jax.experimental.pallas import tpu as pltpu
from jax.sharding import PartitionSpec as P

HD = 64
EPS = 1e-05
BASE = 500000.0
NEG = -1e30
BF = jnp.bfloat16
F32 = jnp.float32
BLOCK = 256
SLOW = 2


def dotf(left, right):
    return jnp.dot(left, right, preferred_element_type=F32)


def dot_t(left, right):
    return lax.dot_general(left, right, (((1,), (1,)), ((), ())), preferred_element_type=F32)


def dot_0(left, right):
    return lax.dot_general(left, right, (((0,), (0,)), ((), ())), preferred_element_type=F32)


def cost(flops, *arrays):
    size = sum(a.size * jnp.dtype(a.dtype).itemsize for a in arrays)
    return pl.CostEstimate(flops=int(flops), bytes_accessed=int(size), transcendentals=0)


def after(value, *others):
    return lax.optimization_barrier((value,) + others)[0]


def swap(value):
    return lax.ppermute(value, "ctx", [(0, 1), (1, 0)])


def pair(mine, theirs, core, axis):
    first = jnp.where(core == 0, mine, theirs)
    second = jnp.where(core == 0, theirs, mine)
    return jnp.concatenate([first, second], axis=axis)


def half_of(value, which, axis):
    size = value.shape[axis] // 2
    return lax.dynamic_slice_in_dim(value, which * size, size, axis)


def xor_pairs(axis, bit):
    return [(k, k ^ bit) for k in range(lax.axis_size(axis))]


def bits_of(axis):
    return [1 << b for b in range(lax.axis_size(axis).bit_length() - 1)]


def gated(value, gate):
    return value if gate is None else after(value, gate)


def near_far():
    return xor_pairs("tp", 1), xor_pairs("tp", 2)


def halved(values, pairs):
    half = values[0].shape[0] // 2
    sent = jnp.concatenate([v[half:].astype(BF) for v in values], axis=0)
    return [v[:half] for v in values], lax.ppermute(sent, "tp", pairs), sent


def summed(kept, got):
    half = kept[0].shape[0]
    return [
        k.astype(F32) + got[n * half : (n + 1) * half].astype(F32) for n, k in enumerate(kept)
    ]


def across(value, *gate):
    near, far = near_far()
    value = after(value, *gate) if gate else value
    both = jnp.concatenate([value, lax.ppermute(value, "tp", far)], axis=0)
    return jnp.concatenate([both, lax.ppermute(both, "tp", near)], axis=0)


def position(index, place, count):
    distance = index ^ place
    result = distance & 0
    for bit in range(count.bit_length() - 1):
        result = result * 2 + ((distance >> bit) & 1)
    return result


def arrange(parts, place_at, kind, back):
    count = lax.axis_size("tp")
    rows = parts[0].shape[0]
    size = rows // count
    width = parts[0].shape[1]
    columns = width // 4

    def kernel(place_ref, *refs):
        out_ref = refs[-1]
        for n in range(len(parts)):
            for j in range(count):
                natural = slice(j * size, (j + 1) * size)
                at = pl.multiple_of(position(j, place_ref[0], count) * size, size)
                if back:
                    out_ref[n * rows + j * size : n * rows + (j + 1) * size, :] = refs[n][
                        pl.ds(at, size), :
                    ].astype(kind)
                else:
                    to = pl.ds(pl.multiple_of(n * rows + at, size), size)
                    out_ref[to, :] = refs[n][natural, :].astype(kind)

    return pl.pallas_call(
        kernel,
        grid_spec=pltpu.PrefetchScalarGridSpec(
            num_scalar_prefetch=1,
            grid=(4,),
            in_specs=[pl.BlockSpec((rows, columns), lambda i, at: (0, i)) for _ in parts],
            out_specs=pl.BlockSpec((rows * len(parts), columns), lambda i, at: (0, i)),
        ),
        out_shape=jax.ShapeDtypeStruct((rows * len(parts), width), kind),
        cost_estimate=cost(0, *parts, *parts),
        name="arrange",
    )(place_at, *parts)


class Scatter:
    def __init__(self, grad):
        self.plain = grad.shape[0] != 4
        if self.plain:
            self.whole = lax.psum_scatter(grad, "fsdp", scatter_dimension=0, tiled=False)
            self.first_sent = grad
            return
        me = lax.axis_index("fsdp")
        cut = grad.shape[1] // 32 * 16
        self.near, self.far = xor_pairs("fsdp", 1), xor_pairs("fsdp", 2)
        self.top, self.low = slice(0, cut), slice(cut, None)
        self.blocks = [lax.dynamic_index_in_dim(grad, me ^ k, 0, keepdims=False) for k in range(4)]
        one, two, three = self.blocks[1:]
        to_near = jnp.stack([one[self.top], three[self.top]])
        to_far = jnp.stack([two[self.low], three[self.low]])
        self.first_sent = to_far + to_near
        self.by_near = lax.ppermute(to_near, "fsdp", self.near)
        self.by_far = lax.ppermute(to_far, "fsdp", self.far)

    def second(self, *gate):
        if self.plain:
            self.token = self.whole
            return
        by_near, by_far = lax.optimization_barrier((self.by_near, self.by_far) + gate)[:2]
        own, one, two = [b.astype(F32) for b in self.blocks[:3]]
        self.a_own = own[self.top] + by_near[0].astype(F32)
        self.b_own = own[self.low] + by_far[0].astype(F32)
        a_far = (two[self.top] + by_near[1].astype(F32)).astype(BF)
        b_near = (one[self.low] + by_far[1].astype(F32)).astype(BF)
        self.token = b_near
        self.a_got = lax.ppermute(a_far, "fsdp", self.far)
        self.b_got = lax.ppermute(b_near, "fsdp", self.near)

    def third(self, *gate):
        if self.plain:
            return self.whole
        a, b = lax.optimization_barrier((self.a_got, self.b_got) + gate)[:2]
        return jnp.concatenate(
            [(self.a_own + a.astype(F32)).astype(BF), (self.b_own + b.astype(F32)).astype(BF)], axis=0
        )


class Gather:
    def __init__(self, shard, axis=0):
        self.shard, self.axis, self.plain = shard, axis, lax.axis_size("fsdp") != 4

    def first(self, *gate):
        shard = after(self.shard, *gate) if gate else self.shard
        if self.plain:
            self.whole = lax.all_gather(shard, "fsdp", axis=self.axis, tiled=True)
            return self.whole
        self.one = lax.ppermute(shard, "fsdp", xor_pairs("fsdp", 1))
        self.two = lax.ppermute(shard, "fsdp", xor_pairs("fsdp", 2))
        return self.two

    def second(self, *gate):
        if self.plain:
            return self.whole
        one, two = self.one, self.two
        if gate:
            one, two = lax.optimization_barrier((one, two) + gate)[:2]
        cut = self.shard.shape[0] // 32 * 16
        far = lax.ppermute(one[:cut], "fsdp", xor_pairs("fsdp", 2))
        near = lax.ppermute(two[cut:], "fsdp", xor_pairs("fsdp", 1))
        return [self.shard, one, two, jnp.concatenate([far, near], axis=0)]


def in_order(pieces, axis, rows=slice(None)):
    if not isinstance(pieces, list):
        count = lax.axis_size("fsdp")
        size = pieces.shape[axis] // count
        pieces = [lax.slice_in_dim(pieces, k * size, (k + 1) * size, axis=axis)[rows] for k in range(count)]
        return jnp.concatenate(pieces, axis=axis)
    me = lax.axis_index("fsdp")
    low, high = (me & 1) == 0, (me & 2) == 0
    own, one, two, three = [p[rows] for p in pieces]
    a, b = jnp.where(low, own, one), jnp.where(low, one, own)
    c, d = jnp.where(low, two, three), jnp.where(low, three, two)
    return jnp.concatenate(
        [jnp.where(high, a, c), jnp.where(high, b, d), jnp.where(high, c, a), jnp.where(high, d, b)],
        axis=axis,
    )


def sum_direct(value, axis, gate):
    if lax.axis_size(axis) > 4:
        return lax.psum(value, axis)
    got = [lax.ppermute(value, axis, xor_pairs(axis, d)) for d in range(1, lax.axis_size(axis))]
    got = lax.optimization_barrier((*got, gate))[:-1]
    for item in got:
        value = value + item
    return value


def grad_kernel(lefts, rights, column, columns, block):
    rows, wide = lefts[0].shape

    def kernel(*refs):
        total = dot_0(refs[0][...], refs[len(lefts)][...])
        for n in range(1, len(lefts)):
            total = total + dot_0(refs[n][...], refs[len(lefts) + n][...])
        refs[-1][...] = total.astype(BF)

    return pl.pallas_call(
        kernel,
        grid=(wide // block,),
        in_specs=[pl.BlockSpec((rows, block), lambda i: (0, i)) for _ in lefts]
        + [pl.BlockSpec((rows, columns), lambda i: (0, column)) for _ in rights],
        out_specs=pl.BlockSpec((block, columns), lambda i: (i, 0)),
        out_shape=jax.ShapeDtypeStruct((wide, columns), BF),
        cost_estimate=cost(SLOW * 2 * len(lefts) * rows * wide * columns, *lefts, *rights),
        name="grad",
    )(*lefts, *rights)


def output_grad(core_at, mine, theirs, dh, shard, fsdp):
    span, wide = mine[0].shape
    if shard % 128:
        grads = []
        for side in (mine, theirs):
            grad = dot_0(jnp.concatenate(side, axis=0), dh).astype(BF).reshape(wide, fsdp, 2, shard)
            grads.append(grad.transpose(1, 0, 2, 3))

        def columns(grad, which):
            return lax.dynamic_index_in_dim(grad, which, 2, keepdims=False)

        return (
            jnp.concatenate([columns(g, core_at[0]) for g in grads], axis=1),
            jnp.concatenate([columns(g, 1 - core_at[0]) for g in grads[::-1]], axis=1),
        )

    def kernel(core_ref, *refs):
        chunks = len(mine)
        keep, send = refs[2 * chunks : 2 * chunks + 2]
        for dh_ref, out_ref, order in ((keep, refs[-2], (0, 1)), (send, refs[-1], (1, 0))):
            for n, side in enumerate(order):
                lefts = refs[side * chunks : (side + 1) * chunks]
                total = dot_0(lefts[0][...], dh_ref[:span])
                for h in range(1, chunks):
                    total = total + dot_0(lefts[h][...], dh_ref[h * span : (h + 1) * span])
                out_ref[0, n * wide : (n + 1) * wide, :] = total.astype(BF)

    part = pl.BlockSpec((1, 2 * wide, shard), lambda f, core: (f, 0, 0))
    return pl.pallas_call(
        kernel,
        grid_spec=pltpu.PrefetchScalarGridSpec(
            num_scalar_prefetch=1,
            grid=(fsdp,),
            in_specs=[pl.BlockSpec((span, wide), lambda f, core: (0, 0))] * (2 * len(mine))
            + [
                pl.BlockSpec((dh.shape[0], shard), lambda f, core: (0, 2 * f + core[0])),
                pl.BlockSpec((dh.shape[0], shard), lambda f, core: (0, 2 * f + 1 - core[0])),
            ],
            out_specs=(part, part),
        ),
        out_shape=(jax.ShapeDtypeStruct((fsdp, 2 * wide, shard), BF),) * 2,
        cost_estimate=cost(SLOW * 4 * dh.size * wide, dh, dh, dh),
        name="output_grad",
    )(core_at, *mine, *theirs, dh, dh)


def halves_swapped(tile):
    lane = lax.broadcasted_iota(jnp.int32, tile.shape, 1)
    width = tile.shape[1]
    back = pltpu.roll(tile, width - HD // 2, 1)
    ahead = pltpu.roll(tile, HD // 2, 1)
    return jnp.where(lane % HD < HD // 2, back, ahead)


def padded(kv):
    lane = lax.broadcasted_iota(jnp.int32, kv.shape, 1)
    low = lane < HD
    other = pltpu.roll(kv, HD, 1)
    zero = jnp.zeros_like(kv)
    keys = (jnp.where(low, kv, zero), jnp.where(low, zero, other))
    vals = (jnp.where(low, other, zero), jnp.where(low, zero, kv))
    return [k.astype(BF) for k in keys], [v.astype(BF) for v in vals]


def causal_mask():
    row = lax.broadcasted_iota(jnp.int32, (BLOCK, BLOCK), 0)
    col = lax.broadcasted_iota(jnp.int32, (BLOCK, BLOCK), 1)
    return col <= row


def spread(ref, base, place, count, lanes, value):
    size = value.shape[0] // count
    for j in range(count):
        at = pl.multiple_of(base + position(j, place, count) * size, size)
        ref[pl.ds(at, size), lanes] = value[j * size : (j + 1) * size]


def collect(ref, base, place, count, lanes, rows):
    size = rows // count
    return jnp.concatenate(
        [
            ref[pl.ds(pl.multiple_of(base + position(j, place, count) * size, size), size), lanes]
            for j in range(count)
        ],
        axis=0,
    )


def attend_blocks(at_ref, q_ref, keys, vals, out_ref, lse_ref, blocks, count):
    core, place = at_ref[0], at_ref[1]
    width = out_ref.shape[1]
    scale = HD ** (-0.5)
    causal = causal_mask()
    for n, i in enumerate(blocks):
        at = slice(i * BLOCK, (i + 1) * BLOCK)
        to = slice(n * BLOCK, (n + 1) * BLOCK)
        for j in range(width // 128):
            lanes = slice(j * 128, (j + 1) * 128)
            queries = q_ref[at, lanes]
            result = None
            for side in range(2):
                key, val = keys[side], vals[side]
                diag = dot_t(queries, key[at]) * scale
                diag = jnp.where(causal, diag, NEG)
                top = jnp.max(diag, axis=-1, keepdims=True)
                if i:
                    past = dot_t(queries, key[: i * BLOCK]) * scale
                    top = jnp.maximum(top, jnp.max(past, axis=-1, keepdims=True))
                    weight = jnp.exp(past - top)
                p_diag = jnp.exp(diag - top)
                total = jnp.sum(p_diag, axis=-1, keepdims=True)
                if i:
                    total = total + jnp.sum(weight, axis=-1, keepdims=True)
                inverse = 1.0 / total
                part = dotf(p_diag.astype(BF), val[at])
                if i:
                    part = part + dotf(weight.astype(BF), val[: i * BLOCK])
                part = part * inverse
                result = part if result is None else result + part
                head = 2 * j + side
                lse_ref[to, head : head + 1] = top + jnp.log(total)
            spread(out_ref, (core ^ n) * BLOCK, place, count, lanes, result.astype(BF))


SCALARS = pl.BlockSpec(memory_space=pltpu.SMEM)


def attend_first(at, qkv, tables, blocks, count):
    tokens, width = qkv.shape
    width = width - 2 * HD
    local = tokens // 2

    def kernel(at_ref, qkv_ref, cos_ref, sin_ref, cos_kv_ref, sin_kv_ref, q_ref, kv_ref, out_ref, lse_ref):
        core = at_ref[0]
        for half in range(2):
            to = slice(half * local, (half + 1) * local)
            source = pl.ds(pl.multiple_of((core ^ half) * local, local), local)
            for j in range(width // 128):
                tile = qkv_ref[source, j * 128 : (j + 1) * 128]
                turned = tile * cos_ref[to] + halves_swapped(tile) * sin_ref[to]
                q_ref[to, j * 128 : (j + 1) * 128] = turned.astype(BF)
            tile = qkv_ref[source, width : width + 128]
            turned = tile * cos_kv_ref[to] + halves_swapped(tile) * sin_kv_ref[to]
            kv_ref[to, :] = turned.astype(BF)
        keys, vals = padded(kv_ref[...].astype(F32))
        attend_blocks(at_ref, q_ref, keys, vals, out_ref, lse_ref, blocks, count)

    rows = len(blocks) * BLOCK
    return pl.pallas_call(
        kernel,
        in_specs=[SCALARS] + [pl.BlockSpec()] * 5,
        out_shape=(
            jax.ShapeDtypeStruct((tokens, width), BF),
            jax.ShapeDtypeStruct((tokens, 2 * HD), BF),
            jax.ShapeDtypeStruct((rows, width), BF),
            jax.ShapeDtypeStruct((rows, width // HD), F32),
        ),
        cost_estimate=cost(SLOW * 4e9, qkv),
        name="attend_first",
    )(at, qkv, *tables)


def attend_next(at, queries, kv, blocks, count):
    width = queries.shape[1]

    def kernel(at_ref, q_ref, kv_ref, out_ref, lse_ref):
        keys, vals = padded(kv_ref[...].astype(F32))
        attend_blocks(at_ref, q_ref, keys, vals, out_ref, lse_ref, blocks, count)

    rows = len(blocks) * BLOCK
    return pl.pallas_call(
        kernel,
        in_specs=[SCALARS] + [pl.BlockSpec()] * 2,
        out_shape=(
            jax.ShapeDtypeStruct((rows, width), BF),
            jax.ShapeDtypeStruct((rows, width // HD), F32),
        ),
        cost_estimate=cost(SLOW * 2.5e9, queries),
        name="attend_next",
    )(at, queries, kv)


def attend_back(at, queries, kv, out, grads, lse, tables, blocks, carried, count):
    tokens, width = queries.shape
    scale = HD ** (-0.5)
    tiles = width // 128
    last = carried is not None

    def kernel(at_ref, q_ref, kv_ref, out_ref, mine_ref, theirs_ref, lse_ref, cos_ref, sin_ref, cos_kv_ref, sin_kv_ref, *refs):
        if last:
            dk_in, dv_in, dq_ref, dq_to_ref, dkv_ref, dkv_to_ref, dk_ref, dv_ref = refs
        else:
            dq_ref, dq_to_ref, dk_ref, dv_ref = refs
        core, place = at_ref[0], at_ref[1]
        keys, vals = padded(kv_ref[...].astype(F32))
        causal = causal_mask()
        low = lax.broadcasted_iota(jnp.int32, (BLOCK, 128), 1) < HD
        if last:
            dk_ref[...] = dk_in[...]
            dv_ref[...] = dv_in[...]
        else:
            dk_ref[...] = jnp.zeros_like(dk_ref)
            dv_ref[...] = jnp.zeros_like(dv_ref)
        for n, i in enumerate(blocks):
            at = slice(i * BLOCK, (i + 1) * BLOCK)
            to = slice(n * BLOCK, (n + 1) * BLOCK)
            for j in range(tiles):
                lanes = slice(j * 128, (j + 1) * 128)
                query = q_ref[at, lanes]
                mine = collect(mine_ref, 0, place, count, lanes, BLOCK).astype(F32)
                theirs = collect(theirs_ref, 0, place, count, lanes, BLOCK).astype(F32)
                grad_f = jnp.where(core == n, mine, theirs)
                grad = grad_f.astype(BF)
                result = collect(out_ref, (core ^ n) * BLOCK, place, count, lanes, BLOCK)
                product = grad_f * result.astype(F32)
                d_query = None
                for side in range(2):
                    key, val = keys[side], vals[side]
                    head = 2 * j + side
                    top = lse_ref[to, head : head + 1]
                    part_of = low if side == 0 else jnp.logical_not(low)
                    delta = jnp.sum(jnp.where(part_of, product, 0.0), axis=-1, keepdims=True)
                    spans = [(at, True)]
                    if i:
                        spans.append((slice(0, i * BLOCK), False))
                    for span, masked in spans:
                        scores = dot_t(query, key[span]) * scale
                        if masked:
                            scores = jnp.where(causal, scores, NEG)
                        probs = jnp.exp(scores - top)
                        d_probs = dot_t(grad, val[span])
                        d_scores = (probs * (d_probs - delta) * scale).astype(BF)
                        dv_ref[side, span] += dot_0(probs.astype(BF), grad)
                        dk_ref[side, span] += dot_0(d_scores, query)
                        part = dotf(d_scores, key[span])
                        d_query = part if d_query is None else d_query + part
                turned = d_query * cos_ref[at] - halves_swapped(d_query) * sin_ref[at]
                turned = turned.astype(BF)
                dq_ref[pl.ds(pl.multiple_of((core ^ n) * BLOCK, BLOCK), BLOCK), lanes] = turned
                spread(dq_to_ref, (core ^ n) * BLOCK, place, count, lanes, turned)
        if last:
            full = lax.broadcasted_iota(jnp.int32, (tokens, 128), 1) < HD
            d_key = dk_ref[0] + pltpu.roll(dk_ref[1], HD, 1)
            d_val = dv_ref[1] + pltpu.roll(dv_ref[0], HD, 1)
            tile = jnp.where(full, d_key, d_val)
            turned = tile * cos_kv_ref[...] - halves_swapped(tile) * sin_kv_ref[...]
            turned = turned.astype(BF)
            half = tokens // 2
            for c in range(2):
                base = (core ^ c) * half
                dkv_ref[pl.ds(pl.multiple_of(base, half), half), :] = turned[c * half : (c + 1) * half]
                for i in range(half // BLOCK):
                    rows = turned[c * half + i * BLOCK : c * half + (i + 1) * BLOCK]
                    spread(dkv_to_ref, base + i * BLOCK, place, count, slice(0, 128), rows)

    sums = [((2, tokens, 128), F32)] * 2
    rows = len(blocks) * BLOCK
    shapes = [jax.ShapeDtypeStruct((rows, width), BF)] * 2
    if last:
        shapes += [jax.ShapeDtypeStruct((tokens, 2 * HD), BF)] * 2
    else:
        shapes += [jax.ShapeDtypeStruct(*s) for s in sums]
    return pl.pallas_call(
        kernel,
        in_specs=[SCALARS] + [pl.BlockSpec()] * (10 + 2 * last),
        out_shape=tuple(shapes),
        scratch_shapes=[pltpu.VMEM(*s) for s in sums] if last else [],
        cost_estimate=cost(SLOW * 4e9, queries, queries),
        name="attend_back",
    )(at, queries, kv, out, *grads, lse, *tables, *(carried or ()))


def rotary_tables(tokens):
    lane = lax.broadcasted_iota(jnp.int32, (1, 2 * HD), 1)
    inverse = BASE ** (-((lane % (HD // 2)).astype(F32) * 2.0) / HD)
    angle = lax.broadcasted_iota(jnp.int32, (tokens, 2 * HD), 0).astype(F32) * inverse
    cosine, sine = jnp.cos(angle), jnp.sin(angle) * jnp.where(lane % HD < HD // 2, -1.0, 1.0)
    keyed = lane < HD
    return (cosine, sine, jnp.where(keyed, cosine, 1.0), jnp.where(keyed, sine, 0.0))


def inverse_rms(rows):
    return lax.rsqrt(jnp.mean(rows * rows, axis=-1, keepdims=True) + EPS)


def norm_backward(rows, scale, gain, grad):
    weighted = grad * gain
    d_rows = scale * weighted - rows * scale**3 * jnp.mean(weighted * rows, axis=-1, keepdims=True)
    return (d_rows, jnp.sum(grad * rows * scale, axis=0))


def stack(*parts):
    return jnp.concatenate(parts, axis=0)


CHUNKS = 2


def body(
    block_input, cotangent, w_query, w_key, w_value, w_output, w_gate, w_up, w_down, attn_gain, ffn_gain
):
    core = lax.axis_index("ctx")
    place = lax.axis_index("tp")
    slot = lax.axis_index("fsdp")
    count = lax.axis_size("tp")
    fsdp = lax.axis_size("fsdp")
    near, far = near_far()
    rows = block_input[0]
    cot = cotangent[0]
    local, width = rows.shape
    shard = w_query.shape[0]
    other = 1 - core
    span = local // CHUNKS
    piece = span // count
    units = w_gate.shape[1] // 2
    where = jnp.stack([core, place]).astype(jnp.int32)
    place_at = place.astype(jnp.int32).reshape(1)

    gains = jnp.concatenate([attn_gain, ffn_gain])
    narrow = (w_query.shape[1] + 2 * w_key.shape[1]) // 2
    lines = -(-gains.shape[0] // (16 * narrow)) * 16
    gain_rows = jnp.pad(gains, (0, lines * narrow - gains.shape[0])).reshape(lines, narrow)

    def packed(which):
        halves = [half_of(w, which, 1) for w in (w_query, w_key, w_value)]
        return stack(jnp.concatenate(halves, axis=1), gain_rows)

    def packed_gu(which):
        return jnp.concatenate([half_of(w_gate, which, 1), half_of(w_up, which, 1)], axis=1)

    qkv_mine, qkv_got = packed(core), swap(packed(other))
    qkv_shard = stack(
        pair(qkv_mine[:shard], qkv_got[:shard], core, 0), pair(qkv_mine[shard:], qkv_got[shard:], core, 0)
    )
    get_qkv = Gather(qkv_shard)
    get_wo = Gather(w_output, 1)
    t_qkv = get_qkv.first()
    gu_got = swap(after(packed_gu(other), qkv_shard))
    gu_shard = pair(packed_gu(core), gu_got, core, 0)
    rows_theirs = swap(after(rows, gu_shard))
    wd_got = swap(after(half_of(w_down, other, 0), rows_theirs))
    wd_shard = pair(half_of(w_down, core, 0), wd_got, core, 1)
    w_gu = lax.all_gather(gu_shard, "fsdp", axis=0, tiled=True)
    wd = lax.all_gather(wd_shard, "fsdp", axis=1, tiled=True)
    scale_own, scale_theirs = inverse_rms(rows), inverse_rms(rows_theirs)
    tables = rotary_tables(2 * local)
    cot_gated = after(cot.astype(BF), rows_theirs)
    cot_own = arrange([cot_gated[h * span : (h + 1) * span] for h in range(CHUNKS)], place_at, BF, False)
    cot_theirs = swap(cot_own)
    qkv_pieces = get_qkv.second(scale_own, scale_theirs, cot_own)
    w_qkv = in_order(qkv_pieces, 0, slice(0, 2 * shard))
    gain_all = in_order(qkv_pieces, 0, slice(2 * shard, None)).reshape(-1, lines * narrow)
    w_qkv, gain_all = lax.optimization_barrier((w_qkv, gain_all, wd_shard) + tuple(tables))[:2]
    get_wo.first(gain_all)
    wo_column = across(w_output, gain_all)
    gain_a = gain_all[:, :shard].reshape(-1).astype(F32)
    gain_f = gain_all[:, shard : 2 * shard].reshape(-1).astype(F32)

    normed = stack(
        (rows * scale_own * gain_a).astype(BF), (rows_theirs * scale_theirs * gain_a).astype(BF)
    )
    qkv = dotf(normed, w_qkv)
    blocks = [[h * span // BLOCK, h * span // BLOCK + local // BLOCK] for h in range(CHUNKS)]
    queries, kv, attn_0, lse_0 = attend_first(where, qkv, tables, blocks[0], count)
    kv = after(kv, wo_column)
    wo_all = lax.all_gather(after(wo_column, wd), ("fsdp", "ctx"), axis=1, tiled=True)

    wo_mine = in_order(get_wo.second(qkv), 1)
    wo_theirs = swap(wo_mine)
    wo_halves = [w.reshape(w.shape[0], -1, shard) for w in (wo_mine, wo_theirs)]
    first = jnp.where(core == 0, wo_halves[0], wo_halves[1])
    second = jnp.where(core == 0, wo_halves[1], wo_halves[0])
    wo = jnp.stack([first, second], axis=2).reshape(w_output.shape[0], width)
    wo_a, wo_b = lax.optimization_barrier((half_of(wo, core, 0), half_of(wo, other, 0)))

    def slice_of(value, h):
        return lax.dynamic_slice_in_dim(value, h * span + place * piece, piece, 0)

    attn_1, lse_1 = attend_next(where, queries, kv, blocks[1], count)
    attn, lse = [attn_0, attn_1], [lse_0, lse_1]
    attn_own = [(a[:span], swap(a[span:])) for a in attn]
    partial = [dotf(attn_own[0][0], wo_a) + dotf(attn_own[0][1], wo_b)]

    def hidden_of(h, total):
        hidden = slice_of(rows, h) + total
        scale = inverse_rms(hidden)
        return hidden, scale, (hidden * scale * gain_f).astype(BF)

    k0, g0, t0 = halved([partial[0]], near)
    partial.append(dotf(after(attn_own[1][0], t0), wo_a) + dotf(attn_own[1][1], wo_b))
    k1, g1, t1 = halved([partial[1]], near)
    v0 = summed(k0, after(g0, t1))
    k0, g0, t0 = halved(v0, far)
    v1 = summed(k1, after(g1, t0))
    k1, g1, t1 = halved(v1, far)
    hidden_0, scale_0, c0 = hidden_of(0, summed(k0, after(g0, t1))[0])
    a0 = lax.ppermute(c0, "tp", far)
    hidden_1, scale_1, c1 = hidden_of(1, summed(k1, after(g1, c0))[0])
    a1 = lax.ppermute(c1, "tp", far)
    cur0 = stack(c0, after(a0, c1))
    b0, s0 = lax.ppermute(cur0, "tp", near), swap(cur0)
    cur1 = stack(c1, after(a1, cur0))
    b1, s1 = lax.ppermute(cur1, "tp", near), swap(cur1)

    cots = [
        stack(cot_own[h * span : (h + 1) * span], cot_theirs[h * span : (h + 1) * span])
        for h in range(CHUNKS)
    ]

    def backward_of(gu, d_inner):
        gate, up = gu[:, :units], gu[:, units:]
        sigma = jax.nn.sigmoid(gate)
        active = gate * sigma
        d_gate = (d_inner * up * sigma * (1.0 + gate * (1.0 - sigma))).astype(BF)
        d_up = (d_inner * active).astype(BF)
        return (active * up).astype(BF), jnp.concatenate([d_gate, d_up], axis=1)

    b0 = after(b0, cur1, *cots)
    hnorm_0 = stack(cur0, b0, s0, swap(b0))
    gu_0 = dotf(hnorm_0, w_gu)
    b1 = after(b1, gu_0)
    s_b1 = swap(b1)
    inner_0, d_gu_0 = backward_of(gu_0, dot_t(cots[0], wd))
    d_full_0 = dot_t(d_gu_0, w_gu)
    s0 = swap(d_full_0[span:].astype(BF))
    cur1, b1, s1, s_b1 = lax.optimization_barrier((cur1, b1, s1, s_b1, d_full_0))[:4]
    hnorm_1 = stack(cur1, b1, s1, s_b1)
    gu_1 = dotf(hnorm_1, w_gu)
    d0 = d_full_0[:span] + after(s0, gu_1).astype(F32)
    k0, g0, t0 = halved([d0], near)
    inner_1, d_gu_1 = backward_of(gu_1, dot_t(after(cots[1], t0), wd))
    v0 = summed(k0, after(g0, d_gu_1))
    k0, g0, t0 = halved(v0, far)
    d_full_1 = dot_t(after(d_gu_1, t0), w_gu)
    s1 = swap(d_full_1[span:].astype(BF))
    d1 = d_full_1[:span] + s1.astype(F32)
    k1, g1, t1 = halved([d1], near)

    def reduced(grad, axis):
        return lax.psum_scatter(grad, "fsdp", scatter_dimension=axis, tiled=True)

    def gradient(lefts, rights, column, *gate):
        n = len(rights)
        rights = lax.optimization_barrier(tuple(rights) + gate)[:n]
        return grad_kernel(lefts, rights, column, units if column is not None else width, 512)

    d_gu, inner, hnorm = [d_gu_0, d_gu_1], [inner_0, inner_1], [hnorm_0, hnorm_1]
    def back_of(h, hidden, scale, total):
        d_norm, gain = norm_backward(hidden, scale, gain_f, total)
        d_hidden = slice_of(cot, h) + d_norm
        return d_hidden, gain, d_hidden.astype(BF)

    heads = w_output.shape[0]

    def to_heads(piece):
        blocks = [piece[:, n * heads : (n + 1) * heads] for n in range(count)]
        distances = [0, 2, 1, 3]
        return blocks[:1] + [
            lax.ppermute(b, "tp", xor_pairs("tp", d)) for b, d in zip(blocks[1:], distances[1:])
        ]

    def grads_of(pieces, *gate):
        pieces = lax.optimization_barrier(tuple(pieces) + gate)[: len(pieces)]
        full = stack(*pieces)
        return half_of(full, core, 1), swap(half_of(full, other, 1))

    dh_0, gain_0, c0 = back_of(0, hidden_0, scale_0, summed(k0, after(g0, t1))[0])
    p0 = dot_t(c0, wo_all).astype(BF)
    x0 = to_heads(p0)
    g_gate = gradient(hnorm, d_gu, 0, *x0[:1], p0)
    v1 = summed(k1, after(g1, g_gate))
    k1, g1, t1 = halved(v1, far)
    g_up = gradient(hnorm, d_gu, 1, t1)
    dh_1, gain_1, c1 = back_of(1, hidden_1, scale_1, summed(k1, after(g1, g_up))[0])
    p1 = dot_t(c1, wo_all).astype(BF)
    x1 = to_heads(p1)
    g_ffn = gain_0 + gain_1
    c_dh = after(stack(c0, c1), p1)
    a_dh = lax.ppermute(c_dh, "tp", far)
    dq_0, dq_to_0, *carried = attend_back(
        where, queries, kv, attn_0, grads_of(x0, g_up, p1), lse_0, tables, blocks[0], None, count
    )
    grads_1 = grads_of(x1, dq_0)
    dq_1, dq_to_1, d_kv, d_kv_to = attend_back(
        where, queries, kv, attn_1, grads_1, lse_1, tables, blocks[1], carried, count
    )

    cur_dh = stack(c_dh, after(a_dh, dq_1))
    b_dh = lax.ppermute(cur_dh, "tp", near)
    dq_to_0, dq_to_1 = lax.optimization_barrier((dq_to_0, dq_to_1, cur_dh))[:2]

    def joined(query, kv_of, h, side):
        at = side * local + h * span
        return jnp.concatenate([query[side * span : (side + 1) * span], kv_of[at : at + span]], axis=1)

    parts = [
        dot_t(stack(*[joined(q, d_kv_to, h, s) for s in range(2)]), w_qkv)
        for h, q in enumerate((dq_to_0, dq_to_1))
    ]
    sent = [swap(p[span:].astype(BF)) for p in parts]
    d0 = parts[0][:span] + sent[0].astype(F32)
    d1 = parts[1][:span] + sent[1].astype(F32)
    k0, g0, t0 = halved([d0], near)
    k1, g1, t1 = halved([d1], near)
    down = [dotf(i, wd) for i in lax.optimization_barrier(tuple(inner) + (t0, t1))[:2]]
    s_down = swap(stack(*[d[span:].astype(BF) for d in down]))
    g_down = grad_kernel(inner, lax.optimization_barrier(tuple(cots) + (*down, b_dh))[:2], 0, width, 512)
    r_gate, r_up, r_down = reduced(g_gate, 0), reduced(g_up, 0), reduced(g_down, 1)
    down = [
        d[:span] + after(s_down, g_down)[n * span : (n + 1) * span].astype(F32) for n, d in enumerate(down)
    ]
    v0 = summed(k0, after(g0, g_down))
    k0, g0, t0 = halved(v0, far)
    r_gate, r_up = lax.optimization_barrier((r_gate, r_up, t0))[:2]
    s_gate = pair(half_of(r_gate, core, 0), swap(half_of(r_gate, other, 0)), core, 1).astype(F32)
    s_up = pair(half_of(r_up, core, 0), swap(half_of(r_up, other, 0)), core, 1).astype(F32)
    v1 = summed(k1, after(g1, t0, s_gate, s_up))
    k1, g1, t1 = halved(v1, far)
    k_out, g_out, t_out = halved(down, near)
    d_qkv = stack(*[joined(q, d_kv, h, s) for s in range(2) for h, q in enumerate((dq_0, dq_1))])
    g_qkv = dot_0(normed, after(d_qkv, t0, t1, t_out)).astype(BF)

    def input_of(h, d_hidden, total):
        d_rows, gain = norm_backward(slice_of(rows, h), slice_of(scale_own, h), gain_a, total)
        return gain, (d_hidden + d_rows).astype(BF)

    by_distance = stack(cur_dh, after(b_dh, t1, t_out)).reshape(count, CHUNKS, piece, width)
    dh_all = by_distance.swapaxes(0, 1).reshape(-1, width)
    keep, send = output_grad(
        core.astype(jnp.int32).reshape(1), [a[0] for a in attn_own], [a[1] for a in attn_own], dh_all, shard, fsdp
    )
    g_output = (keep.astype(F32) + swap(send).astype(F32)).astype(BF)
    g_qkv = g_qkv.reshape(fsdp, -1, narrow)
    joint = g_qkv.shape[1] == g_output.shape[1]
    if joint:
        reduce = [Scatter(jnp.concatenate([g_qkv, g_output], axis=2))]
    else:
        reduce = [Scatter(g_qkv), Scatter(g_output)]
    firsts = [item.first_sent for item in reduce]

    gain_0, c0 = input_of(0, dh_0, summed(k0, after(g0, g_qkv, g_output, *firsts))[0])
    a0 = lax.ppermute(c0, "tp", far)
    gain_1, c1 = input_of(1, dh_1, summed(k1, after(g1, c0))[0])
    a1 = lax.ppermute(c1, "tp", far)
    for item in reduce:
        item.second(c1)
    tokens = [r.token for r in reduce]
    cur0 = stack(c0, after(a0, *tokens))
    b0 = lax.ppermute(cur0, "tp", near)
    v_out = summed(k_out, after(g_out, cur0))
    k_out, g_out, t_out = halved(v_out, far)
    b0 = after(b0, t_out)
    cur1 = stack(c1, after(a1, b0))
    b1 = lax.ppermute(cur1, "tp", near)
    totals = summed(k_out, after(g_out, cur1))
    c_out = stack(hidden_0 + totals[0], hidden_1 + totals[1]).astype(BF)
    a_out = lax.ppermute(c_out, "tp", far)
    g_all = sum_direct(jnp.stack([gain_0 + gain_1, g_ffn]), "ctx", cur0)
    g_all = sum_direct(g_all, "fsdp", c_out)

    r_down = after(r_down, c_out)
    s_down = pair(half_of(r_down, core, 1), swap(half_of(r_down, other, 1)), core, 0).astype(F32)
    results = [item.third(c_out) for item in reduce]
    if joint:
        r_qkv, r_output = results[0][:, :narrow], results[0][:, narrow:]
    else:
        r_qkv, r_output = results
    half = r_output.shape[0] // 2
    s_output = pair(r_output[:half], r_output[half:], core, 0).astype(F32)
    mine, theirs = half_of(r_qkv, core, 0), swap(half_of(r_qkv, other, 0))
    bounds = [0, w_query.shape[1] // 2, (w_query.shape[1] + w_key.shape[1]) // 2, narrow]
    s_query, s_key, s_value = [
        pair(mine[:, a:b], theirs[:, a:b], core, 1).astype(F32) for a, b in zip(bounds, bounds[1:])
    ]
    a_out = after(a_out, b1, s_down, s_query, s_key, s_value, s_output, g_all)
    cur_out = stack(*[stack(c_out[h * piece : (h + 1) * piece], a_out[h * piece : (h + 1) * piece]) for h in range(CHUNKS)])
    b_out = lax.ppermute(cur_out, "tp", near)
    b0, b1 = lax.optimization_barrier((b0, b1, cur_out))[:2]
    d_input = arrange([stack(cur0, b0), stack(cur1, b1)], place_at, F32, True)
    b_out = after(b_out, d_input)
    g_all = sum_direct(g_all, "tp", d_input)
    cur_half, got_half = cur_out.shape[0] // CHUNKS, b_out.shape[0] // CHUNKS
    out = arrange(
        [
            stack(cur_out[h * cur_half : (h + 1) * cur_half], b_out[h * got_half : (h + 1) * got_half])
            for h in range(CHUNKS)
        ],
        place_at,
        F32,
        True,
    )

    start = (slot * 2 + core) * shard
    s_attn = lax.dynamic_slice_in_dim(g_all[0], start, shard, 0)
    s_ffn = lax.dynamic_slice_in_dim(g_all[1], start, shard, 0)
    return (
        out[None],
        d_input[None],
        s_query,
        s_key,
        s_value,
        s_output,
        s_gate,
        s_up,
        s_down,
        s_attn,
        s_ffn,
    )


def solution(mesh):
    placed = (
        P("fsdp", "ctx", None),
        P("fsdp", "ctx", None),
        P(("fsdp", "ctx"), "tp"),
        P(("fsdp", "ctx"), "tp"),
        P(("fsdp", "ctx"), "tp"),
        P("tp", ("fsdp", "ctx")),
        P(("fsdp", "ctx"), "tp"),
        P(("fsdp", "ctx"), "tp"),
        P("tp", ("fsdp", "ctx")),
        P(("fsdp", "ctx")),
        P(("fsdp", "ctx")),
    )
    return jax.shard_map(
        body,
        mesh=mesh,
        in_specs=placed,
        out_specs=(
            P("fsdp", "ctx", None),
            P("fsdp", "ctx", None),
            P(("fsdp", "ctx"), "tp"),
            P(("fsdp", "ctx"), "tp"),
            P(("fsdp", "ctx"), "tp"),
            P("tp", ("fsdp", "ctx")),
            P(("fsdp", "ctx"), "tp"),
            P(("fsdp", "ctx"), "tp"),
            P("tp", ("fsdp", "ctx")),
            P(("fsdp", "ctx")),
            P(("fsdp", "ctx")),
        ),
        check_vma=False,
    )
```

```python
import jax
import jax.numpy as jnp
from jax import lax
from jax.experimental import pallas as pl
from jax.experimental.pallas import tpu as pltpu
from jax.sharding import PartitionSpec as P

HD = 64
EPS = 1e-05
BASE = 500000.0
NEG = -1e30
BF = jnp.bfloat16
F32 = jnp.float32
BLOCK = 256
SLOW = 2


def dotf(left, right):
    return jnp.dot(left, right, preferred_element_type=F32)


def dot_t(left, right):
    return lax.dot_general(left, right, (((1,), (1,)), ((), ())), preferred_element_type=F32)


def dot_0(left, right):
    return lax.dot_general(left, right, (((0,), (0,)), ((), ())), preferred_element_type=F32)


def cost(flops, *arrays):
    size = sum(a.size * jnp.dtype(a.dtype).itemsize for a in arrays)
    return pl.CostEstimate(flops=int(flops), bytes_accessed=int(size), transcendentals=0)


def after(value, *others):
    return lax.optimization_barrier((value,) + others)[0]


def swap(value):
    return lax.ppermute(value, "ctx", [(0, 1), (1, 0)])


def pair(mine, theirs, core, axis):
    first = jnp.where(core == 0, mine, theirs)
    second = jnp.where(core == 0, theirs, mine)
    return jnp.concatenate([first, second], axis=axis)


def half_of(value, which, axis):
    size = value.shape[axis] // 2
    return lax.dynamic_slice_in_dim(value, which * size, size, axis)


def xor_pairs(axis, bit):
    return [(k, k ^ bit) for k in range(lax.axis_size(axis))]


def bits_of(axis):
    return [1 << b for b in range(lax.axis_size(axis).bit_length() - 1)]


def gated(value, gate):
    return value if gate is None else after(value, gate)


def near_far():
    return xor_pairs("tp", 1), xor_pairs("tp", 2)


def halved(values, pairs):
    half = values[0].shape[0] // 2
    sent = jnp.concatenate([v[half:].astype(BF) for v in values], axis=0)
    return [v[:half] for v in values], lax.ppermute(sent, "tp", pairs), sent


def summed(kept, got):
    half = kept[0].shape[0]
    return [
        k.astype(F32) + got[n * half : (n + 1) * half].astype(F32) for n, k in enumerate(kept)
    ]


def across(value, *gate):
    near, far = near_far()
    value = after(value, *gate) if gate else value
    both = jnp.concatenate([value, lax.ppermute(value, "tp", far)], axis=0)
    return jnp.concatenate([both, lax.ppermute(both, "tp", near)], axis=0)


def position(index, place, count):
    distance = index ^ place
    result = distance & 0
    for bit in range(count.bit_length() - 1):
        result = result * 2 + ((distance >> bit) & 1)
    return result


def arrange(parts, place_at, kind, back):
    count = lax.axis_size("tp")
    rows = parts[0].shape[0]
    size = rows // count
    width = parts[0].shape[1]
    columns = width // 4

    def kernel(place_ref, *refs):
        out_ref = refs[-1]
        for n in range(len(parts)):
            for j in range(count):
                natural = slice(j * size, (j + 1) * size)
                at = pl.multiple_of(position(j, place_ref[0], count) * size, size)
                if back:
                    out_ref[n * rows + j * size : n * rows + (j + 1) * size, :] = refs[n][
                        pl.ds(at, size), :
                    ].astype(kind)
                else:
                    to = pl.ds(pl.multiple_of(n * rows + at, size), size)
                    out_ref[to, :] = refs[n][natural, :].astype(kind)

    return pl.pallas_call(
        kernel,
        grid_spec=pltpu.PrefetchScalarGridSpec(
            num_scalar_prefetch=1,
            grid=(4,),
            in_specs=[pl.BlockSpec((rows, columns), lambda i, at: (0, i)) for _ in parts],
            out_specs=pl.BlockSpec((rows * len(parts), columns), lambda i, at: (0, i)),
        ),
        out_shape=jax.ShapeDtypeStruct((rows * len(parts), width), kind),
        cost_estimate=cost(0, *parts, *parts),
        name="arrange",
    )(place_at, *parts)


class Scatter:
    def __init__(self, grad):
        self.plain = grad.shape[0] != 4
        if self.plain:
            self.whole = lax.psum_scatter(grad, "fsdp", scatter_dimension=0, tiled=False)
            self.first_sent = grad
            return
        me = lax.axis_index("fsdp")
        cut = grad.shape[1] // 32 * 16
        self.near, self.far = xor_pairs("fsdp", 1), xor_pairs("fsdp", 2)
        self.top, self.low = slice(0, cut), slice(cut, None)
        self.blocks = [lax.dynamic_index_in_dim(grad, me ^ k, 0, keepdims=False) for k in range(4)]
        one, two, three = self.blocks[1:]
        to_near = jnp.stack([one[self.top], three[self.top]])
        to_far = jnp.stack([two[self.low], three[self.low]])
        self.first_sent = to_far + to_near
        self.by_near = lax.ppermute(to_near, "fsdp", self.near)
        self.by_far = lax.ppermute(to_far, "fsdp", self.far)

    def second(self, *gate):
        if self.plain:
            self.token = self.whole
            return
        by_near, by_far = lax.optimization_barrier((self.by_near, self.by_far) + gate)[:2]
        own, one, two = [b.astype(F32) for b in self.blocks[:3]]
        self.a_own = own[self.top] + by_near[0].astype(F32)
        self.b_own = own[self.low] + by_far[0].astype(F32)
        a_far = (two[self.top] + by_near[1].astype(F32)).astype(BF)
        b_near = (one[self.low] + by_far[1].astype(F32)).astype(BF)
        self.token = b_near
        self.a_got = lax.ppermute(a_far, "fsdp", self.far)
        self.b_got = lax.ppermute(b_near, "fsdp", self.near)

    def third(self, *gate):
        if self.plain:
            return self.whole
        a, b = lax.optimization_barrier((self.a_got, self.b_got) + gate)[:2]
        return jnp.concatenate(
            [(self.a_own + a.astype(F32)).astype(BF), (self.b_own + b.astype(F32)).astype(BF)], axis=0
        )


class Gather:
    def __init__(self, shard, axis=0):
        self.shard, self.axis, self.plain = shard, axis, lax.axis_size("fsdp") != 4

    def first(self, *gate):
        shard = after(self.shard, *gate) if gate else self.shard
        if self.plain:
            self.whole = lax.all_gather(shard, "fsdp", axis=self.axis, tiled=True)
            return self.whole
        self.one = lax.ppermute(shard, "fsdp", xor_pairs("fsdp", 1))
        self.two = lax.ppermute(shard, "fsdp", xor_pairs("fsdp", 2))
        return self.two

    def second(self, *gate):
        if self.plain:
            return self.whole
        one, two = self.one, self.two
        if gate:
            one, two = lax.optimization_barrier((one, two) + gate)[:2]
        cut = self.shard.shape[0] // 32 * 16
        far = lax.ppermute(one[:cut], "fsdp", xor_pairs("fsdp", 2))
        near = lax.ppermute(two[cut:], "fsdp", xor_pairs("fsdp", 1))
        return [self.shard, one, two, jnp.concatenate([far, near], axis=0)]


def in_order(pieces, axis, rows=slice(None)):
    if not isinstance(pieces, list):
        count = lax.axis_size("fsdp")
        size = pieces.shape[axis] // count
        pieces = [lax.slice_in_dim(pieces, k * size, (k + 1) * size, axis=axis)[rows] for k in range(count)]
        return jnp.concatenate(pieces, axis=axis)
    me = lax.axis_index("fsdp")
    low, high = (me & 1) == 0, (me & 2) == 0
    own, one, two, three = [p[rows] for p in pieces]
    a, b = jnp.where(low, own, one), jnp.where(low, one, own)
    c, d = jnp.where(low, two, three), jnp.where(low, three, two)
    return jnp.concatenate(
        [jnp.where(high, a, c), jnp.where(high, b, d), jnp.where(high, c, a), jnp.where(high, d, b)],
        axis=axis,
    )


def sum_direct(value, axis, gate):
    if lax.axis_size(axis) > 4:
        return lax.psum(value, axis)
    got = [lax.ppermute(value, axis, xor_pairs(axis, d)) for d in range(1, lax.axis_size(axis))]
    got = lax.optimization_barrier((*got, gate))[:-1]
    for item in got:
        value = value + item
    return value


def grad_kernel(lefts, rights, column, columns, block):
    rows, wide = lefts[0].shape

    def kernel(*refs):
        total = dot_0(refs[0][...], refs[len(lefts)][...])
        for n in range(1, len(lefts)):
            total = total + dot_0(refs[n][...], refs[len(lefts) + n][...])
        refs[-1][...] = total.astype(BF)

    return pl.pallas_call(
        kernel,
        grid=(wide // block,),
        in_specs=[pl.BlockSpec((rows, block), lambda i: (0, i)) for _ in lefts]
        + [pl.BlockSpec((rows, columns), lambda i: (0, column)) for _ in rights],
        out_specs=pl.BlockSpec((block, columns), lambda i: (i, 0)),
        out_shape=jax.ShapeDtypeStruct((wide, columns), BF),
        cost_estimate=cost(SLOW * 2 * len(lefts) * rows * wide * columns, *lefts, *rights),
        name="grad",
    )(*lefts, *rights)


def output_grad(core_at, mine, theirs, dh, shard, fsdp):
    span, wide = mine[0].shape
    if shard % 128:
        grads = []
        for side in (mine, theirs):
            grad = dot_0(jnp.concatenate(side, axis=0), dh).astype(BF).reshape(wide, fsdp, 2, shard)
            grads.append(grad.transpose(1, 0, 2, 3))

        def columns(grad, which):
            return lax.dynamic_index_in_dim(grad, which, 2, keepdims=False)

        return (
            jnp.concatenate([columns(g, core_at[0]) for g in grads], axis=1),
            jnp.concatenate([columns(g, 1 - core_at[0]) for g in grads[::-1]], axis=1),
        )

    def kernel(core_ref, *refs):
        chunks = len(mine)
        keep, send = refs[2 * chunks : 2 * chunks + 2]
        for dh_ref, out_ref, order in ((keep, refs[-2], (0, 1)), (send, refs[-1], (1, 0))):
            for n, side in enumerate(order):
                lefts = refs[side * chunks : (side + 1) * chunks]
                total = dot_0(lefts[0][...], dh_ref[:span])
                for h in range(1, chunks):
                    total = total + dot_0(lefts[h][...], dh_ref[h * span : (h + 1) * span])
                out_ref[0, n * wide : (n + 1) * wide, :] = total.astype(BF)

    part = pl.BlockSpec((1, 2 * wide, shard), lambda f, core: (f, 0, 0))
    return pl.pallas_call(
        kernel,
        grid_spec=pltpu.PrefetchScalarGridSpec(
            num_scalar_prefetch=1,
            grid=(fsdp,),
            in_specs=[pl.BlockSpec((span, wide), lambda f, core: (0, 0))] * (2 * len(mine))
            + [
                pl.BlockSpec((dh.shape[0], shard), lambda f, core: (0, 2 * f + core[0])),
                pl.BlockSpec((dh.shape[0], shard), lambda f, core: (0, 2 * f + 1 - core[0])),
            ],
            out_specs=(part, part),
        ),
        out_shape=(jax.ShapeDtypeStruct((fsdp, 2 * wide, shard), BF),) * 2,
        cost_estimate=cost(SLOW * 4 * dh.size * wide, dh, dh, dh),
        name="output_grad",
    )(core_at, *mine, *theirs, dh, dh)


def halves_swapped(tile):
    lane = lax.broadcasted_iota(jnp.int32, tile.shape, 1)
    width = tile.shape[1]
    back = pltpu.roll(tile, width - HD // 2, 1)
    ahead = pltpu.roll(tile, HD // 2, 1)
    return jnp.where(lane % HD < HD // 2, back, ahead)


def padded(kv):
    lane = lax.broadcasted_iota(jnp.int32, kv.shape, 1)
    low = lane < HD
    other = pltpu.roll(kv, HD, 1)
    zero = jnp.zeros_like(kv)
    keys = (jnp.where(low, kv, zero), jnp.where(low, zero, other))
    vals = (jnp.where(low, other, zero), jnp.where(low, zero, kv))
    return [k.astype(BF) for k in keys], [v.astype(BF) for v in vals]


def causal_mask():
    row = lax.broadcasted_iota(jnp.int32, (BLOCK, BLOCK), 0)
    col = lax.broadcasted_iota(jnp.int32, (BLOCK, BLOCK), 1)
    return col <= row


def spread(ref, base, place, count, lanes, value):
    size = value.shape[0] // count
    for j in range(count):
        at = pl.multiple_of(base + position(j, place, count) * size, size)
        ref[pl.ds(at, size), lanes] = value[j * size : (j + 1) * size]


def collect(ref, base, place, count, lanes, rows):
    size = rows // count
    return jnp.concatenate(
        [
            ref[pl.ds(pl.multiple_of(base + position(j, place, count) * size, size), size), lanes]
            for j in range(count)
        ],
        axis=0,
    )


def attend_blocks(at_ref, q_ref, keys, vals, out_ref, lse_ref, blocks, count):
    core, place = at_ref[0], at_ref[1]
    width = out_ref.shape[1]
    scale = HD ** (-0.5)
    causal = causal_mask()
    for n, i in enumerate(blocks):
        at = slice(i * BLOCK, (i + 1) * BLOCK)
        to = slice(n * BLOCK, (n + 1) * BLOCK)
        for j in range(width // 128):
            lanes = slice(j * 128, (j + 1) * 128)
            queries = q_ref[at, lanes]
            result = None
            for side in range(2):
                key, val = keys[side], vals[side]
                diag = dot_t(queries, key[at]) * scale
                diag = jnp.where(causal, diag, NEG)
                top = jnp.max(diag, axis=-1, keepdims=True)
                if i:
                    past = dot_t(queries, key[: i * BLOCK]) * scale
                    top = jnp.maximum(top, jnp.max(past, axis=-1, keepdims=True))
                    weight = jnp.exp(past - top)
                p_diag = jnp.exp(diag - top)
                total = jnp.sum(p_diag, axis=-1, keepdims=True)
                if i:
                    total = total + jnp.sum(weight, axis=-1, keepdims=True)
                inverse = 1.0 / total
                part = dotf(p_diag.astype(BF), val[at])
                if i:
                    part = part + dotf(weight.astype(BF), val[: i * BLOCK])
                part = part * inverse
                result = part if result is None else result + part
                head = 2 * j + side
                lse_ref[to, head : head + 1] = top + jnp.log(total)
            spread(out_ref, (core ^ n) * BLOCK, place, count, lanes, result.astype(BF))


SCALARS = pl.BlockSpec(memory_space=pltpu.SMEM)


def attend_first(at, qkv, tables, blocks, count):
    tokens, width = qkv.shape
    width = width - 2 * HD
    local = tokens // 2

    def kernel(at_ref, qkv_ref, cos_ref, sin_ref, cos_kv_ref, sin_kv_ref, q_ref, kv_ref, out_ref, lse_ref):
        core = at_ref[0]
        for half in range(2):
            to = slice(half * local, (half + 1) * local)
            source = pl.ds(pl.multiple_of((core ^ half) * local, local), local)
            for j in range(width // 128):
                tile = qkv_ref[source, j * 128 : (j + 1) * 128]
                turned = tile * cos_ref[to] + halves_swapped(tile) * sin_ref[to]
                q_ref[to, j * 128 : (j + 1) * 128] = turned.astype(BF)
            tile = qkv_ref[source, width : width + 128]
            turned = tile * cos_kv_ref[to] + halves_swapped(tile) * sin_kv_ref[to]
            kv_ref[to, :] = turned.astype(BF)
        keys, vals = padded(kv_ref[...].astype(F32))
        attend_blocks(at_ref, q_ref, keys, vals, out_ref, lse_ref, blocks, count)

    rows = len(blocks) * BLOCK
    return pl.pallas_call(
        kernel,
        in_specs=[SCALARS] + [pl.BlockSpec()] * 5,
        out_shape=(
            jax.ShapeDtypeStruct((tokens, width), BF),
            jax.ShapeDtypeStruct((tokens, 2 * HD), BF),
            jax.ShapeDtypeStruct((rows, width), BF),
            jax.ShapeDtypeStruct((rows, width // HD), F32),
        ),
        cost_estimate=cost(SLOW * 4e9, qkv),
        name="attend_first",
    )(at, qkv, *tables)


def attend_next(at, queries, kv, blocks, count):
    width = queries.shape[1]

    def kernel(at_ref, q_ref, kv_ref, out_ref, lse_ref):
        keys, vals = padded(kv_ref[...].astype(F32))
        attend_blocks(at_ref, q_ref, keys, vals, out_ref, lse_ref, blocks, count)

    rows = len(blocks) * BLOCK
    return pl.pallas_call(
        kernel,
        in_specs=[SCALARS] + [pl.BlockSpec()] * 2,
        out_shape=(
            jax.ShapeDtypeStruct((rows, width), BF),
            jax.ShapeDtypeStruct((rows, width // HD), F32),
        ),
        cost_estimate=cost(SLOW * 2.5e9, queries),
        name="attend_next",
    )(at, queries, kv)


def attend_back(at, queries, kv, out, grads, lse, tables, blocks, carried, count):
    tokens, width = queries.shape
    scale = HD ** (-0.5)
    tiles = width // 128
    last = carried is not None

    def kernel(at_ref, q_ref, kv_ref, out_ref, mine_ref, theirs_ref, lse_ref, cos_ref, sin_ref, cos_kv_ref, sin_kv_ref, *refs):
        if last:
            dk_in, dv_in, dq_ref, dq_to_ref, dkv_ref, dkv_to_ref, dk_ref, dv_ref = refs
        else:
            dq_ref, dq_to_ref, dk_ref, dv_ref = refs
        core, place = at_ref[0], at_ref[1]
        keys, vals = padded(kv_ref[...].astype(F32))
        causal = causal_mask()
        low = lax.broadcasted_iota(jnp.int32, (BLOCK, 128), 1) < HD
        if last:
            dk_ref[...] = dk_in[...]
            dv_ref[...] = dv_in[...]
        else:
            dk_ref[...] = jnp.zeros_like(dk_ref)
            dv_ref[...] = jnp.zeros_like(dv_ref)
        for n, i in enumerate(blocks):
            at = slice(i * BLOCK, (i + 1) * BLOCK)
            to = slice(n * BLOCK, (n + 1) * BLOCK)
            for j in range(tiles):
                lanes = slice(j * 128, (j + 1) * 128)
                query = q_ref[at, lanes]
                mine = collect(mine_ref, 0, place, count, lanes, BLOCK).astype(F32)
                theirs = collect(theirs_ref, 0, place, count, lanes, BLOCK).astype(F32)
                grad_f = jnp.where(core == n, mine, theirs)
                grad = grad_f.astype(BF)
                result = collect(out_ref, (core ^ n) * BLOCK, place, count, lanes, BLOCK)
                product = grad_f * result.astype(F32)
                d_query = None
                for side in range(2):
                    key, val = keys[side], vals[side]
                    head = 2 * j + side
                    top = lse_ref[to, head : head + 1]
                    part_of = low if side == 0 else jnp.logical_not(low)
                    delta = jnp.sum(jnp.where(part_of, product, 0.0), axis=-1, keepdims=True)
                    spans = [(at, True)]
                    if i:
                        spans.append((slice(0, i * BLOCK), False))
                    for span, masked in spans:
                        scores = dot_t(query, key[span]) * scale
                        if masked:
                            scores = jnp.where(causal, scores, NEG)
                        probs = jnp.exp(scores - top)
                        d_probs = dot_t(grad, val[span])
                        d_scores = (probs * (d_probs - delta) * scale).astype(BF)
                        dv_ref[side, span] += dot_0(probs.astype(BF), grad)
                        dk_ref[side, span] += dot_0(d_scores, query)
                        part = dotf(d_scores, key[span])
                        d_query = part if d_query is None else d_query + part
                turned = d_query * cos_ref[at] - halves_swapped(d_query) * sin_ref[at]
                turned = turned.astype(BF)
                dq_ref[pl.ds(pl.multiple_of((core ^ n) * BLOCK, BLOCK), BLOCK), lanes] = turned
                spread(dq_to_ref, (core ^ n) * BLOCK, place, count, lanes, turned)
        if last:
            full = lax.broadcasted_iota(jnp.int32, (tokens, 128), 1) < HD
            d_key = dk_ref[0] + pltpu.roll(dk_ref[1], HD, 1)
            d_val = dv_ref[1] + pltpu.roll(dv_ref[0], HD, 1)
            tile = jnp.where(full, d_key, d_val)
            turned = tile * cos_kv_ref[...] - halves_swapped(tile) * sin_kv_ref[...]
            turned = turned.astype(BF)
            half = tokens // 2
            for c in range(2):
                base = (core ^ c) * half
                dkv_ref[pl.ds(pl.multiple_of(base, half), half), :] = turned[c * half : (c + 1) * half]
                for i in range(half // BLOCK):
                    rows = turned[c * half + i * BLOCK : c * half + (i + 1) * BLOCK]
                    spread(dkv_to_ref, base + i * BLOCK, place, count, slice(0, 128), rows)

    sums = [((2, tokens, 128), F32)] * 2
    rows = len(blocks) * BLOCK
    shapes = [jax.ShapeDtypeStruct((rows, width), BF)] * 2
    if last:
        shapes += [jax.ShapeDtypeStruct((tokens, 2 * HD), BF)] * 2
    else:
        shapes += [jax.ShapeDtypeStruct(*s) for s in sums]
    return pl.pallas_call(
        kernel,
        in_specs=[SCALARS] + [pl.BlockSpec()] * (10 + 2 * last),
        out_shape=tuple(shapes),
        scratch_shapes=[pltpu.VMEM(*s) for s in sums] if last else [],
        cost_estimate=cost(SLOW * 4e9, queries, queries),
        name="attend_back",
    )(at, queries, kv, out, *grads, lse, *tables, *(carried or ()))


def rotary_tables(tokens):
    lane = lax.broadcasted_iota(jnp.int32, (1, 2 * HD), 1)
    inverse = BASE ** (-((lane % (HD // 2)).astype(F32) * 2.0) / HD)
    angle = lax.broadcasted_iota(jnp.int32, (tokens, 2 * HD), 0).astype(F32) * inverse
    cosine, sine = jnp.cos(angle), jnp.sin(angle) * jnp.where(lane % HD < HD // 2, -1.0, 1.0)
    keyed = lane < HD
    return (cosine, sine, jnp.where(keyed, cosine, 1.0), jnp.where(keyed, sine, 0.0))


def inverse_rms(rows):
    return lax.rsqrt(jnp.mean(rows * rows, axis=-1, keepdims=True) + EPS)


def norm_backward(rows, scale, gain, grad):
    weighted = grad * gain
    d_rows = scale * weighted - rows * scale**3 * jnp.mean(weighted * rows, axis=-1, keepdims=True)
    return (d_rows, jnp.sum(grad * rows * scale, axis=0))


def stack(*parts):
    return jnp.concatenate(parts, axis=0)


CHUNKS = 2


def body(
    block_input, cotangent, w_query, w_key, w_value, w_output, w_gate, w_up, w_down, attn_gain, ffn_gain
):
    core = lax.axis_index("ctx")
    place = lax.axis_index("tp")
    slot = lax.axis_index("fsdp")
    count = lax.axis_size("tp")
    fsdp = lax.axis_size("fsdp")
    near, far = near_far()
    rows = block_input[0]
    cot = cotangent[0]
    local, width = rows.shape
    shard = w_query.shape[0]
    other = 1 - core
    span = local // CHUNKS
    piece = span // count
    units = w_gate.shape[1] // 2
    where = jnp.stack([core, place]).astype(jnp.int32)
    place_at = place.astype(jnp.int32).reshape(1)

    gains = jnp.concatenate([attn_gain, ffn_gain])
    narrow = (w_query.shape[1] + 2 * w_key.shape[1]) // 2
    lines = -(-gains.shape[0] // (16 * narrow)) * 16
    gain_rows = jnp.pad(gains, (0, lines * narrow - gains.shape[0])).reshape(lines, narrow)

    def packed(which):
        halves = [half_of(w, which, 1) for w in (w_query, w_key, w_value)]
        return stack(jnp.concatenate(halves, axis=1), gain_rows)

    def packed_gu(which):
        return jnp.concatenate([half_of(w_gate, which, 1), half_of(w_up, which, 1)], axis=1)

    qkv_mine, qkv_got = packed(core), swap(packed(other))
    qkv_shard = stack(
        pair(qkv_mine[:shard], qkv_got[:shard], core, 0), pair(qkv_mine[shard:], qkv_got[shard:], core, 0)
    )
    get_qkv = Gather(qkv_shard)
    get_wo = Gather(w_output, 1)
    t_qkv = get_qkv.first()
    gu_got = swap(after(packed_gu(other), qkv_shard))
    gu_shard = pair(packed_gu(core), gu_got, core, 0)
    rows_theirs = swap(after(rows, gu_shard))
    wd_got = swap(after(half_of(w_down, other, 0), rows_theirs))
    wd_shard = pair(half_of(w_down, core, 0), wd_got, core, 1)
    w_gu = lax.all_gather(gu_shard, "fsdp", axis=0, tiled=True)
    wd = lax.all_gather(wd_shard, "fsdp", axis=1, tiled=True)
    scale_own, scale_theirs = inverse_rms(rows), inverse_rms(rows_theirs)
    tables = rotary_tables(2 * local)
    cot_gated = after(cot.astype(BF), rows_theirs)
    cot_own = arrange([cot_gated[h * span : (h + 1) * span] for h in range(CHUNKS)], place_at, BF, False)
    cot_theirs = swap(cot_own)
    qkv_pieces = get_qkv.second(scale_own, scale_theirs, cot_own)
    w_qkv = in_order(qkv_pieces, 0, slice(0, 2 * shard))
    gain_all = in_order(qkv_pieces, 0, slice(2 * shard, None)).reshape(-1, lines * narrow)
    w_qkv, gain_all = lax.optimization_barrier((w_qkv, gain_all, wd_shard) + tuple(tables))[:2]
    get_wo.first(gain_all)
    wo_column = across(w_output, gain_all)
    gain_a = gain_all[:, :shard].reshape(-1).astype(F32)
    gain_f = gain_all[:, shard : 2 * shard].reshape(-1).astype(F32)

    normed = stack(
        (rows * scale_own * gain_a).astype(BF), (rows_theirs * scale_theirs * gain_a).astype(BF)
    )
    qkv = dotf(normed, w_qkv)
    blocks = [[h * span // BLOCK, h * span // BLOCK + local // BLOCK] for h in range(CHUNKS)]
    queries, kv, attn_0, lse_0 = attend_first(where, qkv, tables, blocks[0], count)
    kv = after(kv, wo_column)
    wo_all = lax.all_gather(after(wo_column, wd), ("fsdp", "ctx"), axis=1, tiled=True)

    wo_mine = in_order(get_wo.second(qkv), 1)
    wo_theirs = swap(wo_mine)
    wo_halves = [w.reshape(w.shape[0], -1, shard) for w in (wo_mine, wo_theirs)]
    first = jnp.where(core == 0, wo_halves[0], wo_halves[1])
    second = jnp.where(core == 0, wo_halves[1], wo_halves[0])
    wo = jnp.stack([first, second], axis=2).reshape(w_output.shape[0], width)
    wo_a, wo_b = lax.optimization_barrier((half_of(wo, core, 0), half_of(wo, other, 0)))

    def slice_of(value, h):
        return lax.dynamic_slice_in_dim(value, h * span + place * piece, piece, 0)

    attn_1, lse_1 = attend_next(where, queries, kv, blocks[1], count)
    attn, lse = [attn_0, attn_1], [lse_0, lse_1]
    attn_own = [(a[:span], swap(a[span:])) for a in attn]
    partial = [dotf(attn_own[0][0], wo_a) + dotf(attn_own[0][1], wo_b)]

    def hidden_of(h, total):
        hidden = slice_of(rows, h) + total
        scale = inverse_rms(hidden)
        return hidden, scale, (hidden * scale * gain_f).astype(BF)

    k0, g0, t0 = halved([partial[0]], near)
    partial.append(dotf(after(attn_own[1][0], t0), wo_a) + dotf(attn_own[1][1], wo_b))
    k1, g1, t1 = halved([partial[1]], near)
    v0 = summed(k0, after(g0, t1))
    k0, g0, t0 = halved(v0, far)
    v1 = summed(k1, after(g1, t0))
    k1, g1, t1 = halved(v1, far)
    hidden_0, scale_0, c0 = hidden_of(0, summed(k0, after(g0, t1))[0])
    a0 = lax.ppermute(c0, "tp", far)
    hidden_1, scale_1, c1 = hidden_of(1, summed(k1, after(g1, c0))[0])
    a1 = lax.ppermute(c1, "tp", far)
    cur0 = stack(c0, after(a0, c1))
    b0, s0 = lax.ppermute(cur0, "tp", near), swap(cur0)
    cur1 = stack(c1, after(a1, cur0))
    b1, s1 = lax.ppermute(cur1, "tp", near), swap(cur1)

    cots = [
        stack(cot_own[h * span : (h + 1) * span], cot_theirs[h * span : (h + 1) * span])
        for h in range(CHUNKS)
    ]

    def backward_of(gu, d_inner):
        gate, up = gu[:, :units], gu[:, units:]
        sigma = jax.nn.sigmoid(gate)
        active = gate * sigma
        d_gate = (d_inner * up * sigma * (1.0 + gate * (1.0 - sigma))).astype(BF)
        d_up = (d_inner * active).astype(BF)
        return (active * up).astype(BF), jnp.concatenate([d_gate, d_up], axis=1)

    b0 = after(b0, cur1, *cots)
    hnorm_0 = stack(cur0, b0, s0, swap(b0))
    gu_0 = dotf(hnorm_0, w_gu)
    b1 = after(b1, gu_0)
    s_b1 = swap(b1)
    inner_0, d_gu_0 = backward_of(gu_0, dot_t(cots[0], wd))
    d_full_0 = dot_t(d_gu_0, w_gu)
    s0 = swap(d_full_0[span:].astype(BF))
    cur1, b1, s1, s_b1 = lax.optimization_barrier((cur1, b1, s1, s_b1, d_full_0))[:4]
    hnorm_1 = stack(cur1, b1, s1, s_b1)
    gu_1 = dotf(hnorm_1, w_gu)
    d0 = d_full_0[:span] + after(s0, gu_1).astype(F32)
    k0, g0, t0 = halved([d0], near)
    inner_1, d_gu_1 = backward_of(gu_1, dot_t(after(cots[1], t0), wd))
    v0 = summed(k0, after(g0, d_gu_1))
    k0, g0, t0 = halved(v0, far)
    d_full_1 = dot_t(after(d_gu_1, t0), w_gu)
    s1 = swap(d_full_1[span:].astype(BF))
    d1 = d_full_1[:span] + s1.astype(F32)
    k1, g1, t1 = halved([d1], near)

    def reduced(grad, axis):
        return lax.psum_scatter(grad, "fsdp", scatter_dimension=axis, tiled=True)

    def gradient(lefts, rights, column, *gate):
        n = len(rights)
        rights = lax.optimization_barrier(tuple(rights) + gate)[:n]
        return grad_kernel(lefts, rights, column, units if column is not None else width, 512)

    d_gu, inner, hnorm = [d_gu_0, d_gu_1], [inner_0, inner_1], [hnorm_0, hnorm_1]
    def back_of(h, hidden, scale, total):
        d_norm, gain = norm_backward(hidden, scale, gain_f, total)
        d_hidden = slice_of(cot, h) + d_norm
        return d_hidden, gain, d_hidden.astype(BF)

    heads = w_output.shape[0]

    def to_heads(piece):
        blocks = [piece[:, n * heads : (n + 1) * heads] for n in range(count)]
        distances = [0, 2, 1, 3]
        return blocks[:1] + [
            lax.ppermute(b, "tp", xor_pairs("tp", d)) for b, d in zip(blocks[1:], distances[1:])
        ]

    def grads_of(pieces, *gate):
        pieces = lax.optimization_barrier(tuple(pieces) + gate)[: len(pieces)]
        full = stack(*pieces)
        return half_of(full, core, 1), swap(half_of(full, other, 1))

    dh_0, gain_0, c0 = back_of(0, hidden_0, scale_0, summed(k0, after(g0, t1))[0])
    p0 = dot_t(c0, wo_all).astype(BF)
    x0 = to_heads(p0)
    g_gate = gradient(hnorm, d_gu, 0, *x0[:1], p0)
    v1 = summed(k1, after(g1, g_gate))
    k1, g1, t1 = halved(v1, far)
    g_up = gradient(hnorm, d_gu, 1, t1)
    dh_1, gain_1, c1 = back_of(1, hidden_1, scale_1, summed(k1, after(g1, g_up))[0])
    p1 = dot_t(c1, wo_all).astype(BF)
    x1 = to_heads(p1)
    g_ffn = gain_0 + gain_1
    c_dh = after(stack(c0, c1), p1)
    a_dh = lax.ppermute(c_dh, "tp", far)
    dq_0, dq_to_0, *carried = attend_back(
        where, queries, kv, attn_0, grads_of(x0, g_up, p1), lse_0, tables, blocks[0], None, count
    )
    grads_1 = grads_of(x1, dq_0)
    dq_1, dq_to_1, d_kv, d_kv_to = attend_back(
        where, queries, kv, attn_1, grads_1, lse_1, tables, blocks[1], carried, count
    )

    cur_dh = stack(c_dh, after(a_dh, dq_1))
    b_dh = lax.ppermute(cur_dh, "tp", near)
    dq_to_0, dq_to_1 = lax.optimization_barrier((dq_to_0, dq_to_1, cur_dh))[:2]

    def joined(query, kv_of, h, side):
        at = side * local + h * span
        return jnp.concatenate([query[side * span : (side + 1) * span], kv_of[at : at + span]], axis=1)

    parts = [
        dot_t(stack(*[joined(q, d_kv_to, h, s) for s in range(2)]), w_qkv)
        for h, q in enumerate((dq_to_0, dq_to_1))
    ]
    sent = [swap(p[span:].astype(BF)) for p in parts]
    d0 = parts[0][:span] + sent[0].astype(F32)
    d1 = parts[1][:span] + sent[1].astype(F32)
    k0, g0, t0 = halved([d0], near)
    k1, g1, t1 = halved([d1], near)
    down = [dotf(i, wd) for i in lax.optimization_barrier(tuple(inner) + (t0, t1))[:2]]
    s_down = swap(stack(*[d[span:].astype(BF) for d in down]))
    g_down = grad_kernel(inner, lax.optimization_barrier(tuple(cots) + (*down, b_dh))[:2], 0, width, 512)
    r_gate, r_up, r_down = reduced(g_gate, 0), reduced(g_up, 0), reduced(g_down, 1)
    down = [
        d[:span] + after(s_down, g_down)[n * span : (n + 1) * span].astype(F32) for n, d in enumerate(down)
    ]
    v0 = summed(k0, after(g0, g_down))
    k0, g0, t0 = halved(v0, far)
    r_gate, r_up = lax.optimization_barrier((r_gate, r_up, t0))[:2]
    s_gate = pair(half_of(r_gate, core, 0), swap(half_of(r_gate, other, 0)), core, 1).astype(F32)
    s_up = pair(half_of(r_up, core, 0), swap(half_of(r_up, other, 0)), core, 1).astype(F32)
    v1 = summed(k1, after(g1, t0, s_gate, s_up))
    k1, g1, t1 = halved(v1, far)
    k_out, g_out, t_out = halved(down, near)
    d_qkv = stack(*[joined(q, d_kv, h, s) for s in range(2) for h, q in enumerate((dq_0, dq_1))])

    def input_of(h, d_hidden, total):
        d_rows, gain = norm_backward(slice_of(rows, h), slice_of(scale_own, h), gain_a, total)
        return gain, (d_hidden + d_rows).astype(BF)

    by_distance = stack(cur_dh, after(b_dh, t1, t_out)).reshape(count, CHUNKS, piece, width)
    dh_all = by_distance.swapaxes(0, 1).reshape(-1, width)
    keep, send = output_grad(
        core.astype(jnp.int32).reshape(1), [a[0] for a in attn_own], [a[1] for a in attn_own], dh_all, shard, fsdp
    )
    gain_0, c0 = input_of(0, dh_0, summed(k0, after(g0, keep))[0])
    a0 = lax.ppermute(c0, "tp", far)
    gain_1, c1 = input_of(1, dh_1, summed(k1, after(g1, c0))[0])
    a1 = lax.ppermute(c1, "tp", far)
    g_qkv = dot_0(normed, after(d_qkv, c0)).astype(BF)
    g_output = (keep.astype(F32) + swap(send).astype(F32)).astype(BF)
    g_qkv = g_qkv.reshape(fsdp, -1, narrow)
    joint = g_qkv.shape[1] == g_output.shape[1]
    if joint:
        reduce = [Scatter(jnp.concatenate([g_qkv, g_output], axis=2))]
    else:
        reduce = [Scatter(g_qkv), Scatter(g_output)]
    firsts = [item.first_sent for item in reduce]

    for item in reduce:
        item.second(c1, *firsts)
    tokens = [r.token for r in reduce]
    cur0 = stack(c0, after(a0, *tokens))
    b0 = lax.ppermute(cur0, "tp", near)
    v_out = summed(k_out, after(g_out, cur0))
    k_out, g_out, t_out = halved(v_out, far)
    b0 = after(b0, t_out)
    cur1 = stack(c1, after(a1, b0))
    b1 = lax.ppermute(cur1, "tp", near)
    totals = summed(k_out, after(g_out, cur1))
    c_out = stack(hidden_0 + totals[0], hidden_1 + totals[1]).astype(BF)
    a_out = lax.ppermute(c_out, "tp", far)
    g_all = sum_direct(jnp.stack([gain_0 + gain_1, g_ffn]), "ctx", cur0)
    g_all = sum_direct(g_all, "fsdp", c_out)

    r_down = after(r_down, c_out)
    s_down = pair(half_of(r_down, core, 1), swap(half_of(r_down, other, 1)), core, 0).astype(F32)
    results = [item.third(c_out) for item in reduce]
    if joint:
        r_qkv, r_output = results[0][:, :narrow], results[0][:, narrow:]
    else:
        r_qkv, r_output = results
    half = r_output.shape[0] // 2
    s_output = pair(r_output[:half], r_output[half:], core, 0).astype(F32)
    mine, theirs = half_of(r_qkv, core, 0), swap(half_of(r_qkv, other, 0))
    bounds = [0, w_query.shape[1] // 2, (w_query.shape[1] + w_key.shape[1]) // 2, narrow]
    s_query, s_key, s_value = [
        pair(mine[:, a:b], theirs[:, a:b], core, 1).astype(F32) for a, b in zip(bounds, bounds[1:])
    ]
    a_out = after(a_out, b1, s_down, s_query, s_key, s_value, s_output, g_all)
    cur_out = stack(*[stack(c_out[h * piece : (h + 1) * piece], a_out[h * piece : (h + 1) * piece]) for h in range(CHUNKS)])
    b_out = lax.ppermute(cur_out, "tp", near)
    b0, b1 = lax.optimization_barrier((b0, b1, cur_out))[:2]
    d_input = arrange([stack(cur0, b0), stack(cur1, b1)], place_at, F32, True)
    b_out = after(b_out, d_input)
    g_all = sum_direct(g_all, "tp", d_input)
    cur_half, got_half = cur_out.shape[0] // CHUNKS, b_out.shape[0] // CHUNKS
    out = arrange(
        [
            stack(cur_out[h * cur_half : (h + 1) * cur_half], b_out[h * got_half : (h + 1) * got_half])
            for h in range(CHUNKS)
        ],
        place_at,
        F32,
        True,
    )

    start = (slot * 2 + core) * shard
    s_attn = lax.dynamic_slice_in_dim(g_all[0], start, shard, 0)
    s_ffn = lax.dynamic_slice_in_dim(g_all[1], start, shard, 0)
    return (
        out[None],
        d_input[None],
        s_query,
        s_key,
        s_value,
        s_output,
        s_gate,
        s_up,
        s_down,
        s_attn,
        s_ffn,
    )


def solution(mesh):
    placed = (
        P("fsdp", "ctx", None),
        P("fsdp", "ctx", None),
        P(("fsdp", "ctx"), "tp"),
        P(("fsdp", "ctx"), "tp"),
        P(("fsdp", "ctx"), "tp"),
        P("tp", ("fsdp", "ctx")),
        P(("fsdp", "ctx"), "tp"),
        P(("fsdp", "ctx"), "tp"),
        P("tp", ("fsdp", "ctx")),
        P(("fsdp", "ctx")),
        P(("fsdp", "ctx")),
    )
    return jax.shard_map(
        body,
        mesh=mesh,
        in_specs=placed,
        out_specs=(
            P("fsdp", "ctx", None),
            P("fsdp", "ctx", None),
            P(("fsdp", "ctx"), "tp"),
            P(("fsdp", "ctx"), "tp"),
            P(("fsdp", "ctx"), "tp"),
            P("tp", ("fsdp", "ctx")),
            P(("fsdp", "ctx"), "tp"),
            P(("fsdp", "ctx"), "tp"),
            P("tp", ("fsdp", "ctx")),
            P(("fsdp", "ctx")),
            P(("fsdp", "ctx")),
        ),
        check_vma=False,
    )
```

```python
import jax
import jax.numpy as jnp
from jax import lax
from jax.experimental import pallas as pl
from jax.experimental.pallas import tpu as pltpu
from jax.sharding import PartitionSpec as P

HD = 64
EPS = 1e-05
BASE = 500000.0
NEG = -1e30
BF = jnp.bfloat16
F32 = jnp.float32
BLOCK = 256
SLOW = 2


def dotf(left, right):
    return jnp.dot(left, right, preferred_element_type=F32)


def dot_t(left, right):
    return lax.dot_general(left, right, (((1,), (1,)), ((), ())), preferred_element_type=F32)


def dot_0(left, right):
    return lax.dot_general(left, right, (((0,), (0,)), ((), ())), preferred_element_type=F32)


def cost(flops, *arrays):
    size = sum(a.size * jnp.dtype(a.dtype).itemsize for a in arrays)
    return pl.CostEstimate(flops=int(flops), bytes_accessed=int(size), transcendentals=0)


def after(value, *others):
    return lax.optimization_barrier((value,) + others)[0]


def swap(value):
    return lax.ppermute(value, "ctx", [(0, 1), (1, 0)])


def pair(mine, theirs, core, axis):
    first = jnp.where(core == 0, mine, theirs)
    second = jnp.where(core == 0, theirs, mine)
    return jnp.concatenate([first, second], axis=axis)


def half_of(value, which, axis):
    size = value.shape[axis] // 2
    return lax.dynamic_slice_in_dim(value, which * size, size, axis)


def xor_pairs(axis, bit):
    return [(k, k ^ bit) for k in range(lax.axis_size(axis))]


def bits_of(axis):
    return [1 << b for b in range(lax.axis_size(axis).bit_length() - 1)]


def gated(value, gate):
    return value if gate is None else after(value, gate)


def near_far():
    return xor_pairs("tp", 1), xor_pairs("tp", 2)


def halved(values, pairs):
    half = values[0].shape[0] // 2
    sent = jnp.concatenate([v[half:].astype(BF) for v in values], axis=0)
    return [v[:half] for v in values], lax.ppermute(sent, "tp", pairs), sent


def summed(kept, got):
    half = kept[0].shape[0]
    return [
        k.astype(F32) + got[n * half : (n + 1) * half].astype(F32) for n, k in enumerate(kept)
    ]


def across(value, *gate):
    near, far = near_far()
    value = after(value, *gate) if gate else value
    both = jnp.concatenate([value, lax.ppermute(value, "tp", far)], axis=0)
    return jnp.concatenate([both, lax.ppermute(both, "tp", near)], axis=0)


def position(index, place, count):
    distance = index ^ place
    result = distance & 0
    for bit in range(count.bit_length() - 1):
        result = result * 2 + ((distance >> bit) & 1)
    return result


def arrange(parts, place_at, kind, back):
    count = lax.axis_size("tp")
    rows = parts[0].shape[0]
    size = rows // count
    width = parts[0].shape[1]
    columns = width // 4

    def kernel(place_ref, *refs):
        out_ref = refs[-1]
        for n in range(len(parts)):
            for j in range(count):
                natural = slice(j * size, (j + 1) * size)
                at = pl.multiple_of(position(j, place_ref[0], count) * size, size)
                if back:
                    out_ref[n * rows + j * size : n * rows + (j + 1) * size, :] = refs[n][
                        pl.ds(at, size), :
                    ].astype(kind)
                else:
                    to = pl.ds(pl.multiple_of(n * rows + at, size), size)
                    out_ref[to, :] = refs[n][natural, :].astype(kind)

    return pl.pallas_call(
        kernel,
        grid_spec=pltpu.PrefetchScalarGridSpec(
            num_scalar_prefetch=1,
            grid=(4,),
            in_specs=[pl.BlockSpec((rows, columns), lambda i, at: (0, i)) for _ in parts],
            out_specs=pl.BlockSpec((rows * len(parts), columns), lambda i, at: (0, i)),
        ),
        out_shape=jax.ShapeDtypeStruct((rows * len(parts), width), kind),
        cost_estimate=cost(0, *parts, *parts),
        name="arrange",
    )(place_at, *parts)


class Scatter:
    def __init__(self, grad):
        self.plain = grad.shape[0] != 4
        if self.plain:
            self.whole = lax.psum_scatter(grad, "fsdp", scatter_dimension=0, tiled=False)
            self.first_sent = grad
            return
        me = lax.axis_index("fsdp")
        cut = grad.shape[1] // 32 * 16
        self.near, self.far = xor_pairs("fsdp", 1), xor_pairs("fsdp", 2)
        self.top, self.low = slice(0, cut), slice(cut, None)
        self.blocks = [lax.dynamic_index_in_dim(grad, me ^ k, 0, keepdims=False) for k in range(4)]
        one, two, three = self.blocks[1:]
        to_near = jnp.stack([one[self.top], three[self.top]])
        to_far = jnp.stack([two[self.low], three[self.low]])
        self.first_sent = to_far + to_near
        self.by_near = lax.ppermute(to_near, "fsdp", self.near)
        self.by_far = lax.ppermute(to_far, "fsdp", self.far)

    def second(self, *gate):
        if self.plain:
            self.token = self.whole
            return
        by_near, by_far = lax.optimization_barrier((self.by_near, self.by_far) + gate)[:2]
        own, one, two = [b.astype(F32) for b in self.blocks[:3]]
        self.a_own = own[self.top] + by_near[0].astype(F32)
        self.b_own = own[self.low] + by_far[0].astype(F32)
        a_far = (two[self.top] + by_near[1].astype(F32)).astype(BF)
        b_near = (one[self.low] + by_far[1].astype(F32)).astype(BF)
        self.token = b_near
        self.a_got = lax.ppermute(a_far, "fsdp", self.far)
        self.b_got = lax.ppermute(b_near, "fsdp", self.near)

    def third(self, *gate):
        if self.plain:
            return self.whole
        a, b = lax.optimization_barrier((self.a_got, self.b_got) + gate)[:2]
        return jnp.concatenate(
            [(self.a_own + a.astype(F32)).astype(BF), (self.b_own + b.astype(F32)).astype(BF)], axis=0
        )


class Gather:
    def __init__(self, shard, axis=0):
        self.shard, self.axis, self.plain = shard, axis, lax.axis_size("fsdp") != 4

    def first(self, *gate):
        shard = after(self.shard, *gate) if gate else self.shard
        if self.plain:
            self.whole = lax.all_gather(shard, "fsdp", axis=self.axis, tiled=True)
            return self.whole
        self.one = lax.ppermute(shard, "fsdp", xor_pairs("fsdp", 1))
        self.two = lax.ppermute(shard, "fsdp", xor_pairs("fsdp", 2))
        return self.two

    def second(self, *gate):
        if self.plain:
            return self.whole
        one, two = self.one, self.two
        if gate:
            one, two = lax.optimization_barrier((one, two) + gate)[:2]
        cut = self.shard.shape[0] // 32 * 16
        far = lax.ppermute(one[:cut], "fsdp", xor_pairs("fsdp", 2))
        near = lax.ppermute(two[cut:], "fsdp", xor_pairs("fsdp", 1))
        return [self.shard, one, two, jnp.concatenate([far, near], axis=0)]


def in_order(pieces, axis, rows=slice(None)):
    if not isinstance(pieces, list):
        count = lax.axis_size("fsdp")
        size = pieces.shape[axis] // count
        pieces = [lax.slice_in_dim(pieces, k * size, (k + 1) * size, axis=axis)[rows] for k in range(count)]
        return jnp.concatenate(pieces, axis=axis)
    me = lax.axis_index("fsdp")
    low, high = (me & 1) == 0, (me & 2) == 0
    own, one, two, three = [p[rows] for p in pieces]
    a, b = jnp.where(low, own, one), jnp.where(low, one, own)
    c, d = jnp.where(low, two, three), jnp.where(low, three, two)
    return jnp.concatenate(
        [jnp.where(high, a, c), jnp.where(high, b, d), jnp.where(high, c, a), jnp.where(high, d, b)],
        axis=axis,
    )


def sum_direct(value, axis, gate):
    if lax.axis_size(axis) > 4:
        return lax.psum(value, axis)
    got = [lax.ppermute(value, axis, xor_pairs(axis, d)) for d in range(1, lax.axis_size(axis))]
    got = lax.optimization_barrier((*got, gate))[:-1]
    for item in got:
        value = value + item
    return value


def grad_kernel(lefts, rights, column, columns, block):
    rows, wide = lefts[0].shape

    def kernel(*refs):
        total = dot_0(refs[0][...], refs[len(lefts)][...])
        for n in range(1, len(lefts)):
            total = total + dot_0(refs[n][...], refs[len(lefts) + n][...])
        refs[-1][...] = total.astype(BF)

    return pl.pallas_call(
        kernel,
        grid=(wide // block,),
        in_specs=[pl.BlockSpec((rows, block), lambda i: (0, i)) for _ in lefts]
        + [pl.BlockSpec((rows, columns), lambda i: (0, column)) for _ in rights],
        out_specs=pl.BlockSpec((block, columns), lambda i: (i, 0)),
        out_shape=jax.ShapeDtypeStruct((wide, columns), BF),
        cost_estimate=cost(SLOW * 2 * len(lefts) * rows * wide * columns, *lefts, *rights),
        name="grad",
    )(*lefts, *rights)


def output_grad(core_at, mine, theirs, dh, shard, fsdp):
    span, wide = mine[0].shape
    if shard % 128:
        grads = []
        for side in (mine, theirs):
            grad = dot_0(jnp.concatenate(side, axis=0), dh).astype(BF).reshape(wide, fsdp, 2, shard)
            grads.append(grad.transpose(1, 0, 2, 3))

        def columns(grad, which):
            return lax.dynamic_index_in_dim(grad, which, 2, keepdims=False)

        return (
            jnp.concatenate([columns(g, core_at[0]) for g in grads], axis=1),
            jnp.concatenate([columns(g, 1 - core_at[0]) for g in grads[::-1]], axis=1),
        )

    def kernel(core_ref, *refs):
        chunks = len(mine)
        keep, send = refs[2 * chunks : 2 * chunks + 2]
        for dh_ref, out_ref, order in ((keep, refs[-2], (0, 1)), (send, refs[-1], (1, 0))):
            for n, side in enumerate(order):
                lefts = refs[side * chunks : (side + 1) * chunks]
                total = dot_0(lefts[0][...], dh_ref[:span])
                for h in range(1, chunks):
                    total = total + dot_0(lefts[h][...], dh_ref[h * span : (h + 1) * span])
                out_ref[0, n * wide : (n + 1) * wide, :] = total.astype(BF)

    part = pl.BlockSpec((1, 2 * wide, shard), lambda f, core: (f, 0, 0))
    return pl.pallas_call(
        kernel,
        grid_spec=pltpu.PrefetchScalarGridSpec(
            num_scalar_prefetch=1,
            grid=(fsdp,),
            in_specs=[pl.BlockSpec((span, wide), lambda f, core: (0, 0))] * (2 * len(mine))
            + [
                pl.BlockSpec((dh.shape[0], shard), lambda f, core: (0, 2 * f + core[0])),
                pl.BlockSpec((dh.shape[0], shard), lambda f, core: (0, 2 * f + 1 - core[0])),
            ],
            out_specs=(part, part),
        ),
        out_shape=(jax.ShapeDtypeStruct((fsdp, 2 * wide, shard), BF),) * 2,
        cost_estimate=cost(SLOW * 4 * dh.size * wide, dh, dh, dh),
        name="output_grad",
    )(core_at, *mine, *theirs, dh, dh)


def halves_swapped(tile):
    lane = lax.broadcasted_iota(jnp.int32, tile.shape, 1)
    width = tile.shape[1]
    back = pltpu.roll(tile, width - HD // 2, 1)
    ahead = pltpu.roll(tile, HD // 2, 1)
    return jnp.where(lane % HD < HD // 2, back, ahead)


def padded(kv):
    lane = lax.broadcasted_iota(jnp.int32, kv.shape, 1)
    low = lane < HD
    other = pltpu.roll(kv, HD, 1)
    zero = jnp.zeros_like(kv)
    keys = (jnp.where(low, kv, zero), jnp.where(low, zero, other))
    vals = (jnp.where(low, other, zero), jnp.where(low, zero, kv))
    return [k.astype(BF) for k in keys], [v.astype(BF) for v in vals]


def causal_mask():
    row = lax.broadcasted_iota(jnp.int32, (BLOCK, BLOCK), 0)
    col = lax.broadcasted_iota(jnp.int32, (BLOCK, BLOCK), 1)
    return col <= row


def spread(ref, base, place, count, lanes, value):
    size = value.shape[0] // count
    for j in range(count):
        at = pl.multiple_of(base + position(j, place, count) * size, size)
        ref[pl.ds(at, size), lanes] = value[j * size : (j + 1) * size]


def collect(ref, base, place, count, lanes, rows):
    size = rows // count
    return jnp.concatenate(
        [
            ref[pl.ds(pl.multiple_of(base + position(j, place, count) * size, size), size), lanes]
            for j in range(count)
        ],
        axis=0,
    )


def attend_blocks(at_ref, q_ref, keys, vals, out_ref, lse_ref, blocks, count):
    core, place = at_ref[0], at_ref[1]
    width = out_ref.shape[1]
    scale = HD ** (-0.5)
    causal = causal_mask()
    for n, i in enumerate(blocks):
        at = slice(i * BLOCK, (i + 1) * BLOCK)
        to = slice(n * BLOCK, (n + 1) * BLOCK)
        for j in range(width // 128):
            lanes = slice(j * 128, (j + 1) * 128)
            queries = q_ref[at, lanes]
            result = None
            for side in range(2):
                key, val = keys[side], vals[side]
                diag = dot_t(queries, key[at]) * scale
                diag = jnp.where(causal, diag, NEG)
                top = jnp.max(diag, axis=-1, keepdims=True)
                if i:
                    past = dot_t(queries, key[: i * BLOCK]) * scale
                    top = jnp.maximum(top, jnp.max(past, axis=-1, keepdims=True))
                    weight = jnp.exp(past - top)
                p_diag = jnp.exp(diag - top)
                total = jnp.sum(p_diag, axis=-1, keepdims=True)
                if i:
                    total = total + jnp.sum(weight, axis=-1, keepdims=True)
                inverse = 1.0 / total
                part = dotf(p_diag.astype(BF), val[at])
                if i:
                    part = part + dotf(weight.astype(BF), val[: i * BLOCK])
                part = part * inverse
                result = part if result is None else result + part
                head = 2 * j + side
                lse_ref[to, head : head + 1] = top + jnp.log(total)
            spread(out_ref, (core ^ n) * BLOCK, place, count, lanes, result.astype(BF))


SCALARS = pl.BlockSpec(memory_space=pltpu.SMEM)


def attend_first(at, qkv, tables, blocks, count):
    tokens, width = qkv.shape
    width = width - 2 * HD
    local = tokens // 2

    def kernel(at_ref, qkv_ref, cos_ref, sin_ref, cos_kv_ref, sin_kv_ref, q_ref, kv_ref, out_ref, lse_ref):
        core = at_ref[0]
        for half in range(2):
            to = slice(half * local, (half + 1) * local)
            source = pl.ds(pl.multiple_of((core ^ half) * local, local), local)
            for j in range(width // 128):
                tile = qkv_ref[source, j * 128 : (j + 1) * 128]
                turned = tile * cos_ref[to] + halves_swapped(tile) * sin_ref[to]
                q_ref[to, j * 128 : (j + 1) * 128] = turned.astype(BF)
            tile = qkv_ref[source, width : width + 128]
            turned = tile * cos_kv_ref[to] + halves_swapped(tile) * sin_kv_ref[to]
            kv_ref[to, :] = turned.astype(BF)
        keys, vals = padded(kv_ref[...].astype(F32))
        attend_blocks(at_ref, q_ref, keys, vals, out_ref, lse_ref, blocks, count)

    rows = len(blocks) * BLOCK
    return pl.pallas_call(
        kernel,
        in_specs=[SCALARS] + [pl.BlockSpec()] * 5,
        out_shape=(
            jax.ShapeDtypeStruct((tokens, width), BF),
            jax.ShapeDtypeStruct((tokens, 2 * HD), BF),
            jax.ShapeDtypeStruct((rows, width), BF),
            jax.ShapeDtypeStruct((rows, width // HD), F32),
        ),
        cost_estimate=cost(SLOW * 4e9, qkv),
        name="attend_first",
    )(at, qkv, *tables)


def attend_next(at, queries, kv, blocks, count):
    width = queries.shape[1]

    def kernel(at_ref, q_ref, kv_ref, out_ref, lse_ref):
        keys, vals = padded(kv_ref[...].astype(F32))
        attend_blocks(at_ref, q_ref, keys, vals, out_ref, lse_ref, blocks, count)

    rows = len(blocks) * BLOCK
    return pl.pallas_call(
        kernel,
        in_specs=[SCALARS] + [pl.BlockSpec()] * 2,
        out_shape=(
            jax.ShapeDtypeStruct((rows, width), BF),
            jax.ShapeDtypeStruct((rows, width // HD), F32),
        ),
        cost_estimate=cost(SLOW * 2.5e9, queries),
        name="attend_next",
    )(at, queries, kv)


def attend_back(at, queries, kv, out, grads, lse, tables, blocks, carried, count):
    tokens, width = queries.shape
    scale = HD ** (-0.5)
    tiles = width // 128
    last = carried is not None

    def kernel(at_ref, q_ref, kv_ref, out_ref, mine_ref, theirs_ref, lse_ref, cos_ref, sin_ref, cos_kv_ref, sin_kv_ref, *refs):
        if last:
            dk_in, dv_in, dq_ref, dq_to_ref, dkv_ref, dkv_to_ref, dk_ref, dv_ref = refs
        else:
            dq_ref, dq_to_ref, dk_ref, dv_ref = refs
        core, place = at_ref[0], at_ref[1]
        keys, vals = padded(kv_ref[...].astype(F32))
        causal = causal_mask()
        low = lax.broadcasted_iota(jnp.int32, (BLOCK, 128), 1) < HD
        if last:
            dk_ref[...] = dk_in[...]
            dv_ref[...] = dv_in[...]
        else:
            dk_ref[...] = jnp.zeros_like(dk_ref)
            dv_ref[...] = jnp.zeros_like(dv_ref)
        for n, i in enumerate(blocks):
            at = slice(i * BLOCK, (i + 1) * BLOCK)
            to = slice(n * BLOCK, (n + 1) * BLOCK)
            for j in range(tiles):
                lanes = slice(j * 128, (j + 1) * 128)
                query = q_ref[at, lanes]
                mine = collect(mine_ref, 0, place, count, lanes, BLOCK).astype(F32)
                theirs = collect(theirs_ref, 0, place, count, lanes, BLOCK).astype(F32)
                grad_f = jnp.where(core == n, mine, theirs)
                grad = grad_f.astype(BF)
                result = collect(out_ref, (core ^ n) * BLOCK, place, count, lanes, BLOCK)
                product = grad_f * result.astype(F32)
                d_query = None
                for side in range(2):
                    key, val = keys[side], vals[side]
                    head = 2 * j + side
                    top = lse_ref[to, head : head + 1]
                    part_of = low if side == 0 else jnp.logical_not(low)
                    delta = jnp.sum(jnp.where(part_of, product, 0.0), axis=-1, keepdims=True)
                    spans = [(at, True)]
                    if i:
                        spans.append((slice(0, i * BLOCK), False))
                    for span, masked in spans:
                        scores = dot_t(query, key[span]) * scale
                        if masked:
                            scores = jnp.where(causal, scores, NEG)
                        probs = jnp.exp(scores - top)
                        d_probs = dot_t(grad, val[span])
                        d_scores = (probs * (d_probs - delta) * scale).astype(BF)
                        dv_ref[side, span] += dot_0(probs.astype(BF), grad)
                        dk_ref[side, span] += dot_0(d_scores, query)
                        part = dotf(d_scores, key[span])
                        d_query = part if d_query is None else d_query + part
                turned = d_query * cos_ref[at] - halves_swapped(d_query) * sin_ref[at]
                turned = turned.astype(BF)
                dq_ref[pl.ds(pl.multiple_of((core ^ n) * BLOCK, BLOCK), BLOCK), lanes] = turned
                spread(dq_to_ref, (core ^ n) * BLOCK, place, count, lanes, turned)
        if last:
            full = lax.broadcasted_iota(jnp.int32, (tokens, 128), 1) < HD
            d_key = dk_ref[0] + pltpu.roll(dk_ref[1], HD, 1)
            d_val = dv_ref[1] + pltpu.roll(dv_ref[0], HD, 1)
            tile = jnp.where(full, d_key, d_val)
            turned = tile * cos_kv_ref[...] - halves_swapped(tile) * sin_kv_ref[...]
            turned = turned.astype(BF)
            half = tokens // 2
            for c in range(2):
                base = (core ^ c) * half
                dkv_ref[pl.ds(pl.multiple_of(base, half), half), :] = turned[c * half : (c + 1) * half]
                for i in range(half // BLOCK):
                    rows = turned[c * half + i * BLOCK : c * half + (i + 1) * BLOCK]
                    spread(dkv_to_ref, base + i * BLOCK, place, count, slice(0, 128), rows)

    sums = [((2, tokens, 128), F32)] * 2
    rows = len(blocks) * BLOCK
    shapes = [jax.ShapeDtypeStruct((rows, width), BF)] * 2
    if last:
        shapes += [jax.ShapeDtypeStruct((tokens, 2 * HD), BF)] * 2
    else:
        shapes += [jax.ShapeDtypeStruct(*s) for s in sums]
    return pl.pallas_call(
        kernel,
        in_specs=[SCALARS] + [pl.BlockSpec()] * (10 + 2 * last),
        out_shape=tuple(shapes),
        scratch_shapes=[pltpu.VMEM(*s) for s in sums] if last else [],
        cost_estimate=cost(SLOW * 4e9, queries, queries),
        name="attend_back",
    )(at, queries, kv, out, *grads, lse, *tables, *(carried or ()))


def rotary_tables(tokens):
    lane = lax.broadcasted_iota(jnp.int32, (1, 2 * HD), 1)
    inverse = BASE ** (-((lane % (HD // 2)).astype(F32) * 2.0) / HD)
    angle = lax.broadcasted_iota(jnp.int32, (tokens, 2 * HD), 0).astype(F32) * inverse
    cosine, sine = jnp.cos(angle), jnp.sin(angle) * jnp.where(lane % HD < HD // 2, -1.0, 1.0)
    keyed = lane < HD
    return (cosine, sine, jnp.where(keyed, cosine, 1.0), jnp.where(keyed, sine, 0.0))


def inverse_rms(rows):
    return lax.rsqrt(jnp.mean(rows * rows, axis=-1, keepdims=True) + EPS)


def norm_backward(rows, scale, gain, grad):
    weighted = grad * gain
    d_rows = scale * weighted - rows * scale**3 * jnp.mean(weighted * rows, axis=-1, keepdims=True)
    return (d_rows, jnp.sum(grad * rows * scale, axis=0))


def stack(*parts):
    return jnp.concatenate(parts, axis=0)


CHUNKS = 2


def body(
    block_input, cotangent, w_query, w_key, w_value, w_output, w_gate, w_up, w_down, attn_gain, ffn_gain
):
    core = lax.axis_index("ctx")
    place = lax.axis_index("tp")
    slot = lax.axis_index("fsdp")
    count = lax.axis_size("tp")
    fsdp = lax.axis_size("fsdp")
    near, far = near_far()
    rows = block_input[0]
    cot = cotangent[0]
    local, width = rows.shape
    shard = w_query.shape[0]
    other = 1 - core
    span = local // CHUNKS
    piece = span // count
    units = w_gate.shape[1] // 2
    where = jnp.stack([core, place]).astype(jnp.int32)
    place_at = place.astype(jnp.int32).reshape(1)

    gains = jnp.concatenate([attn_gain, ffn_gain])
    narrow = (w_query.shape[1] + 2 * w_key.shape[1]) // 2
    lines = -(-gains.shape[0] // (16 * narrow)) * 16
    gain_rows = jnp.pad(gains, (0, lines * narrow - gains.shape[0])).reshape(lines, narrow)

    def packed(which):
        halves = [half_of(w, which, 1) for w in (w_query, w_key, w_value)]
        return stack(jnp.concatenate(halves, axis=1), gain_rows)

    def packed_gu(which):
        return jnp.concatenate([half_of(w_gate, which, 1), half_of(w_up, which, 1)], axis=1)

    qkv_mine, qkv_got = packed(core), swap(packed(other))
    qkv_shard = stack(
        pair(qkv_mine[:shard], qkv_got[:shard], core, 0), pair(qkv_mine[shard:], qkv_got[shard:], core, 0)
    )
    get_qkv = Gather(qkv_shard)
    get_wo = Gather(w_output, 1)
    t_qkv = get_qkv.first()
    gu_got = swap(after(packed_gu(other), qkv_shard))
    gu_shard = pair(packed_gu(core), gu_got, core, 0)
    rows_theirs = swap(after(rows, gu_shard))
    wd_got = swap(after(half_of(w_down, other, 0), rows_theirs))
    wd_shard = pair(half_of(w_down, core, 0), wd_got, core, 1)
    w_gu = lax.all_gather(gu_shard, "fsdp", axis=0, tiled=True)
    wd = lax.all_gather(wd_shard, "fsdp", axis=1, tiled=True)
    scale_own, scale_theirs = inverse_rms(rows), inverse_rms(rows_theirs)
    tables = rotary_tables(2 * local)
    cot_gated = after(cot.astype(BF), rows_theirs)
    cot_own = arrange([cot_gated[h * span : (h + 1) * span] for h in range(CHUNKS)], place_at, BF, False)
    cot_theirs = swap(cot_own)
    qkv_pieces = get_qkv.second(scale_own, scale_theirs, cot_own)
    w_qkv = in_order(qkv_pieces, 0, slice(0, 2 * shard))
    gain_all = in_order(qkv_pieces, 0, slice(2 * shard, None)).reshape(-1, lines * narrow)
    w_qkv, gain_all = lax.optimization_barrier((w_qkv, gain_all, wd_shard) + tuple(tables))[:2]
    get_wo.first(gain_all)
    wo_column = across(w_output, gain_all)
    gain_a = gain_all[:, :shard].reshape(-1).astype(F32)
    gain_f = gain_all[:, shard : 2 * shard].reshape(-1).astype(F32)

    normed = stack(
        (rows * scale_own * gain_a).astype(BF), (rows_theirs * scale_theirs * gain_a).astype(BF)
    )
    qkv = dotf(normed, w_qkv)
    blocks = [[h * span // BLOCK, h * span // BLOCK + local // BLOCK] for h in range(CHUNKS)]
    queries, kv, attn_0, lse_0 = attend_first(where, qkv, tables, blocks[0], count)
    kv = after(kv, wo_column)
    wo_all = lax.all_gather(after(wo_column, wd), ("fsdp", "ctx"), axis=1, tiled=True)

    wo_mine = in_order(get_wo.second(qkv), 1)
    wo_theirs = swap(wo_mine)
    wo_halves = [w.reshape(w.shape[0], -1, shard) for w in (wo_mine, wo_theirs)]
    first = jnp.where(core == 0, wo_halves[0], wo_halves[1])
    second = jnp.where(core == 0, wo_halves[1], wo_halves[0])
    wo = jnp.stack([first, second], axis=2).reshape(w_output.shape[0], width)
    wo_a, wo_b = lax.optimization_barrier((half_of(wo, core, 0), half_of(wo, other, 0)))

    def slice_of(value, h):
        return lax.dynamic_slice_in_dim(value, h * span + place * piece, piece, 0)

    attn_1, lse_1 = attend_next(where, queries, kv, blocks[1], count)
    attn, lse = [attn_0, attn_1], [lse_0, lse_1]
    attn_own = [(a[:span], swap(a[span:])) for a in attn]
    partial = [dotf(attn_own[0][0], wo_a) + dotf(attn_own[0][1], wo_b)]

    def hidden_of(h, total):
        hidden = slice_of(rows, h) + total
        scale = inverse_rms(hidden)
        return hidden, scale, (hidden * scale * gain_f).astype(BF)

    k0, g0, t0 = halved([partial[0]], near)
    partial.append(dotf(after(attn_own[1][0], t0), wo_a) + dotf(attn_own[1][1], wo_b))
    k1, g1, t1 = halved([partial[1]], near)
    v0 = summed(k0, after(g0, t1))
    k0, g0, t0 = halved(v0, far)
    v1 = summed(k1, after(g1, t0))
    k1, g1, t1 = halved(v1, far)
    hidden_0, scale_0, c0 = hidden_of(0, summed(k0, after(g0, t1))[0])
    a0 = lax.ppermute(c0, "tp", far)
    hidden_1, scale_1, c1 = hidden_of(1, summed(k1, after(g1, c0))[0])
    a1 = lax.ppermute(c1, "tp", far)
    cur0 = stack(c0, after(a0, c1))
    b0, s0 = lax.ppermute(cur0, "tp", near), swap(cur0)
    cur1 = stack(c1, after(a1, cur0))
    b1, s1 = lax.ppermute(cur1, "tp", near), swap(cur1)

    cots = [
        stack(cot_own[h * span : (h + 1) * span], cot_theirs[h * span : (h + 1) * span])
        for h in range(CHUNKS)
    ]

    def backward_of(gu, d_inner):
        gate, up = gu[:, :units], gu[:, units:]
        sigma = jax.nn.sigmoid(gate)
        active = gate * sigma
        d_gate = (d_inner * up * sigma * (1.0 + gate * (1.0 - sigma))).astype(BF)
        d_up = (d_inner * active).astype(BF)
        return (active * up).astype(BF), jnp.concatenate([d_gate, d_up], axis=1)

    b0 = after(b0, cur1, *cots)
    hnorm_0 = stack(cur0, b0, s0, swap(b0))
    gu_0 = dotf(hnorm_0, w_gu)
    b1 = after(b1, gu_0)
    s_b1 = swap(b1)
    inner_0, d_gu_0 = backward_of(gu_0, dot_t(cots[0], wd))
    d_full_0 = dot_t(d_gu_0, w_gu)
    s0 = swap(d_full_0[span:].astype(BF))
    cur1, b1, s1, s_b1 = lax.optimization_barrier((cur1, b1, s1, s_b1, d_full_0))[:4]
    hnorm_1 = stack(cur1, b1, s1, s_b1)
    gu_1 = dotf(hnorm_1, w_gu)
    d0 = d_full_0[:span] + after(s0, gu_1).astype(F32)
    k0, g0, t0 = halved([d0], near)
    inner_1, d_gu_1 = backward_of(gu_1, dot_t(after(cots[1], t0), wd))
    v0 = summed(k0, after(g0, d_gu_1))
    k0, g0, t0 = halved(v0, far)
    d_full_1 = dot_t(after(d_gu_1, t0), w_gu)
    s1 = swap(d_full_1[span:].astype(BF))
    d1 = d_full_1[:span] + s1.astype(F32)
    k1, g1, t1 = halved([d1], near)

    def reduced(grad, axis):
        return lax.psum_scatter(grad, "fsdp", scatter_dimension=axis, tiled=True)

    def gradient(lefts, rights, column, *gate):
        n = len(rights)
        rights = lax.optimization_barrier(tuple(rights) + gate)[:n]
        return grad_kernel(lefts, rights, column, units if column is not None else width, 512)

    d_gu, inner, hnorm = [d_gu_0, d_gu_1], [inner_0, inner_1], [hnorm_0, hnorm_1]
    def back_of(h, hidden, scale, total):
        d_norm, gain = norm_backward(hidden, scale, gain_f, total)
        d_hidden = slice_of(cot, h) + d_norm
        return d_hidden, gain, d_hidden.astype(BF)

    heads = w_output.shape[0]

    def to_heads(piece):
        blocks = [piece[:, n * heads : (n + 1) * heads] for n in range(count)]
        distances = [0, 2, 1, 3]
        return blocks[:1] + [
            lax.ppermute(b, "tp", xor_pairs("tp", d)) for b, d in zip(blocks[1:], distances[1:])
        ]

    def grads_of(pieces, *gate):
        pieces = lax.optimization_barrier(tuple(pieces) + gate)[: len(pieces)]
        full = stack(*pieces)
        return half_of(full, core, 1), swap(half_of(full, other, 1))

    dh_0, gain_0, c0 = back_of(0, hidden_0, scale_0, summed(k0, after(g0, t1))[0])
    p0 = dot_t(c0, wo_all).astype(BF)
    x0 = to_heads(p0)
    g_gate = gradient(hnorm, d_gu, 0, *x0[:1], p0)
    v1 = summed(k1, after(g1, g_gate))
    k1, g1, t1 = halved(v1, far)
    g_up = gradient(hnorm, d_gu, 1, t1)
    dh_1, gain_1, c1 = back_of(1, hidden_1, scale_1, summed(k1, after(g1, g_up))[0])
    p1 = dot_t(c1, wo_all).astype(BF)
    x1 = to_heads(p1)
    g_ffn = gain_0 + gain_1
    c_dh = after(stack(c0, c1), p1)
    a_dh = lax.ppermute(c_dh, "tp", far)
    dq_0, dq_to_0, *carried = attend_back(
        where, queries, kv, attn_0, grads_of(x0, g_up, p1), lse_0, tables, blocks[0], None, count
    )
    grads_1 = grads_of(x1, dq_0)
    dq_1, dq_to_1, d_kv, d_kv_to = attend_back(
        where, queries, kv, attn_1, grads_1, lse_1, tables, blocks[1], carried, count
    )

    cur_dh = stack(c_dh, after(a_dh, dq_1))
    b_dh = lax.ppermute(cur_dh, "tp", near)
    dq_to_0, dq_to_1 = lax.optimization_barrier((dq_to_0, dq_to_1, cur_dh))[:2]

    def joined(query, kv_of, h, side):
        at = side * local + h * span
        return jnp.concatenate([query[side * span : (side + 1) * span], kv_of[at : at + span]], axis=1)

    parts = [
        dot_t(stack(*[joined(q, d_kv_to, h, s) for s in range(2)]), w_qkv)
        for h, q in enumerate((dq_to_0, dq_to_1))
    ]
    sent = [swap(p[span:].astype(BF)) for p in parts]
    d0 = parts[0][:span] + sent[0].astype(F32)
    d1 = parts[1][:span] + sent[1].astype(F32)
    k0, g0, t0 = halved([d0], near)
    k1, g1, t1 = halved([d1], near)
    d_qkv = stack(*[joined(q, d_kv, h, s) for s in range(2) for h, q in enumerate((dq_0, dq_1))])
    down = [dotf(i, wd) for i in lax.optimization_barrier(tuple(inner) + (t0, t1, d_qkv))[:2]]
    s_down = swap(stack(*[d[span:].astype(BF) for d in down]))
    g_down = grad_kernel(inner, lax.optimization_barrier(tuple(cots) + (*down, b_dh))[:2], 0, width, 512)
    down = [
        d[:span] + after(s_down, g_down)[n * span : (n + 1) * span].astype(F32) for n, d in enumerate(down)
    ]
    v0 = summed(k0, after(g0, g_down))
    k0, g0, t0 = halved(v0, far)
    r_gate, r_up, r_down = reduced(g_gate, 0), reduced(g_up, 0), reduced(after(g_down, t0), 1)
    r_gate, r_up = lax.optimization_barrier((r_gate, r_up, t0))[:2]
    s_gate = pair(half_of(r_gate, core, 0), swap(half_of(r_gate, other, 0)), core, 1).astype(F32)
    s_up = pair(half_of(r_up, core, 0), swap(half_of(r_up, other, 0)), core, 1).astype(F32)
    v1 = summed(k1, after(g1, t0, s_gate, s_up))
    k1, g1, t1 = halved(v1, far)
    k_out, g_out, t_out = halved(down, near)

    def input_of(h, d_hidden, total):
        d_rows, gain = norm_backward(slice_of(rows, h), slice_of(scale_own, h), gain_a, total)
        return gain, (d_hidden + d_rows).astype(BF)

    by_distance = stack(cur_dh, after(b_dh, t1, t_out)).reshape(count, CHUNKS, piece, width)
    dh_all = by_distance.swapaxes(0, 1).reshape(-1, width)
    keep, send = output_grad(
        core.astype(jnp.int32).reshape(1), [a[0] for a in attn_own], [a[1] for a in attn_own], dh_all, shard, fsdp
    )
    gain_0, c0 = input_of(0, dh_0, summed(k0, after(g0, keep))[0])
    a0 = lax.ppermute(c0, "tp", far)
    gain_1, c1 = input_of(1, dh_1, summed(k1, after(g1, c0))[0])
    a1 = lax.ppermute(c1, "tp", far)
    g_qkv = dot_0(normed, after(d_qkv, c0)).astype(BF)
    g_output = (keep.astype(F32) + swap(send).astype(F32)).astype(BF)
    g_qkv = g_qkv.reshape(fsdp, -1, narrow)
    joint = g_qkv.shape[1] == g_output.shape[1]
    if joint:
        reduce = [Scatter(jnp.concatenate([g_qkv, g_output], axis=2))]
    else:
        reduce = [Scatter(g_qkv), Scatter(g_output)]
    firsts = [item.first_sent for item in reduce]

    for item in reduce:
        item.second(c1, *firsts)
    tokens = [r.token for r in reduce]
    cur0 = stack(c0, after(a0, *tokens))
    b0 = lax.ppermute(cur0, "tp", near)
    v_out = summed(k_out, after(g_out, cur0))
    k_out, g_out, t_out = halved(v_out, far)
    b0 = after(b0, t_out)
    cur1 = stack(c1, after(a1, b0))
    b1 = lax.ppermute(cur1, "tp", near)
    totals = summed(k_out, after(g_out, cur1))
    c_out = stack(hidden_0 + totals[0], hidden_1 + totals[1]).astype(BF)
    a_out = lax.ppermute(c_out, "tp", far)
    g_all = sum_direct(jnp.stack([gain_0 + gain_1, g_ffn]), "ctx", cur0)
    g_all = sum_direct(g_all, "fsdp", c_out)

    r_down = after(r_down, c_out)
    s_down = pair(half_of(r_down, core, 1), swap(half_of(r_down, other, 1)), core, 0).astype(F32)
    results = [item.third(c_out) for item in reduce]
    if joint:
        r_qkv, r_output = results[0][:, :narrow], results[0][:, narrow:]
    else:
        r_qkv, r_output = results
    half = r_output.shape[0] // 2
    s_output = pair(r_output[:half], r_output[half:], core, 0).astype(F32)
    mine, theirs = half_of(r_qkv, core, 0), swap(half_of(r_qkv, other, 0))
    bounds = [0, w_query.shape[1] // 2, (w_query.shape[1] + w_key.shape[1]) // 2, narrow]
    s_query, s_key, s_value = [
        pair(mine[:, a:b], theirs[:, a:b], core, 1).astype(F32) for a, b in zip(bounds, bounds[1:])
    ]
    a_out = after(a_out, b1, s_down, s_query, s_key, s_value, s_output, g_all)
    cur_out = stack(*[stack(c_out[h * piece : (h + 1) * piece], a_out[h * piece : (h + 1) * piece]) for h in range(CHUNKS)])
    b_out = lax.ppermute(cur_out, "tp", near)
    b0, b1 = lax.optimization_barrier((b0, b1, cur_out))[:2]
    d_input = arrange([stack(cur0, b0), stack(cur1, b1)], place_at, F32, True)
    b_out = after(b_out, d_input)
    g_all = sum_direct(g_all, "tp", d_input)
    cur_half, got_half = cur_out.shape[0] // CHUNKS, b_out.shape[0] // CHUNKS
    out = arrange(
        [
            stack(cur_out[h * cur_half : (h + 1) * cur_half], b_out[h * got_half : (h + 1) * got_half])
            for h in range(CHUNKS)
        ],
        place_at,
        F32,
        True,
    )

    start = (slot * 2 + core) * shard
    s_attn = lax.dynamic_slice_in_dim(g_all[0], start, shard, 0)
    s_ffn = lax.dynamic_slice_in_dim(g_all[1], start, shard, 0)
    return (
        out[None],
        d_input[None],
        s_query,
        s_key,
        s_value,
        s_output,
        s_gate,
        s_up,
        s_down,
        s_attn,
        s_ffn,
    )


def solution(mesh):
    placed = (
        P("fsdp", "ctx", None),
        P("fsdp", "ctx", None),
        P(("fsdp", "ctx"), "tp"),
        P(("fsdp", "ctx"), "tp"),
        P(("fsdp", "ctx"), "tp"),
        P("tp", ("fsdp", "ctx")),
        P(("fsdp", "ctx"), "tp"),
        P(("fsdp", "ctx"), "tp"),
        P("tp", ("fsdp", "ctx")),
        P(("fsdp", "ctx")),
        P(("fsdp", "ctx")),
    )
    return jax.shard_map(
        body,
        mesh=mesh,
        in_specs=placed,
        out_specs=(
            P("fsdp", "ctx", None),
            P("fsdp", "ctx", None),
            P(("fsdp", "ctx"), "tp"),
            P(("fsdp", "ctx"), "tp"),
            P(("fsdp", "ctx"), "tp"),
            P("tp", ("fsdp", "ctx")),
            P(("fsdp", "ctx"), "tp"),
            P(("fsdp", "ctx"), "tp"),
            P("tp", ("fsdp", "ctx")),
            P(("fsdp", "ctx")),
            P(("fsdp", "ctx")),
        ),
        check_vma=False,
    )
```
